128 devices in a mesh: dp: 8 (over y, core), row: 2 (over z_lo), col: 8 (over x, z_hi).
Axes of the slice: x: 4, y: 4, z: 4 (z_hi: 2, z_lo: 2; z = z_hi * 2 + z_lo), core: 2. Of those that a mesh axis runs over, the one named last changes fastest.
Arguments:
- hidden_in: float32 [2048, 1024], P('dp', 'row'), may hold values from -6 to 6
- cotangent: float32 [2048, 1024], P('dp', 'row'), may hold values from -6 to 6
- norm_gains: float32 [2, 2, 1024], P(None, None, 'row'), may hold values from 0.1 to 1.9
- query_key_value_weight: bfloat16 [2, 1024, 2048], P(None, 'row', 'col'), may hold values from -0.1875 to 0.1875
- w_out: bfloat16 [2, 1024, 1024], P(None, 'col', 'row'), may hold values from -0.75 to 0.75
- w_router: bfloat16 [2, 1024, 32], P(None, 'row', 'col'), may hold values from -0.1875 to 0.1875
- w_gate_up: bfloat16 [2, 32, 1024, 1024], P(None, 'col', 'row'), may hold values from -0.1875 to 0.1875
- w_down: bfloat16 [2, 32, 512, 1024], P(None, 'col', None, 'row'), may hold values from -0.75 to 0.75
- expert_ids: int32 [2, 2048, 8], P(None, 'dp'), may hold values from 0 to 31, all different within a row; in each aligned block of 256 rows (0 to 255, 256 to 511, ..., all dimensions but the last counted through in order) at most 128 rows name the same one
Outputs:
- block_out: float32 [2048, 1024], P('dp', 'row')
- grad_hidden: float32 [2048, 1024], P('dp', 'row')
- grad_gains: float32 [2, 2, 1024], P(None, None, ('row', 'dp'))
- grad_qkv: float32 [2, 1024, 2048], P(None, ('row', 'dp'), 'col')
- grad_out: float32 [2, 1024, 1024], P(None, ('col', 'dp'), 'row')
- grad_router: float32 [2, 1024, 32], P(None, ('row', 'dp'), 'col')
- grad_gate_up: float32 [2, 32, 1024, 1024], P(None, 'col', ('row', 'dp'))
- grad_down: float32 [2, 32, 512, 1024], P(None, 'col', 'dp', 'row')
The draws below stay inside these ranges and needn't reach their ends.
Inputs may be any that keep to these rules, and one draw needn't show every extreme that they name: `expert_ids`: each token names 8 different experts in each layer. Among the 256 tokens of one index of dp in one layer, no expert is named by more than 128 tokens, a bound that some block reaches.
All inputs are finite; a program needn't handle non-finite values.
Results may differ from the reference program's by a relative error of at most 0.04.
Values may be sent and summed in bfloat16 or wider, within the bound.
No kernel may reach another device: no remote copies, remote signals or barrier semaphores. Data moves between devices by JAX's collectives and lax.ppermute only.
A program may use at most 128 MiB of HBM per device.

```python
import math
import jax
import jax.numpy as jnp
import numpy as np
from jax import lax

MODEL_WIDTH = 1024
QUERY_HEADS = 16
KEY_VALUE_HEADS = 8
HEAD_SIZE = 64
E = 32
TOP = 8
FF = 512
LAYER_COUNT = 2
SEQUENCE_TOKENS = 256
TOK_DEV = 256
TOTAL_TOKENS = 2048
CAP = 128
QUERY_PER_GROUP = 2
N_DP = 8


def steps_of(rng, extent, cuts, least, largest):
    gain, own = 1.0, jax.random.fold_in(rng, 6)
    for position, shards_of in cuts:
        heights = jnp.exp(jax.random.uniform(jax.random.fold_in(own, position), (shards_of,), jnp.float32, least / len(cuts), largest / len(cuts)))
        gain = gain * jnp.repeat(heights, extent[position] // shards_of).reshape([-1 if axis == position else 1 for axis in range(len(extent))])
    return gain


def deal_out(key, own, number, rows, amount, top, reach, lean):
    sequence = jax.random.permutation(key, amount)
    crowded, usual = shares(amount, rows * top, reach, lean, True), shares(amount, rows * top, reach, lean, False)
    places = jnp.arange(amount)

    def named(sizes, rotation):
        used = int((sizes > 0).sum())
        fixed = max(1, used // 4)
        passed = fixed + (places - fixed + rotation * (used - fixed)) % max(1, amount - fixed)
        return jnp.zeros((amount,), jnp.int32).at[sequence[jnp.where(places < fixed, places, passed)]].set(jnp.asarray(sizes, jnp.int32))

    sizes = jnp.where(number % 4 == 0, named(crowded, number // 4), named(usual, number - number // 4 - 1))
    mixed = jax.random.permutation(jax.random.fold_in(own, 3), amount)
    giver, taker = mixed[0:amount // 2 * 2:2], mixed[1:amount // 2 * 2:2]
    margin = jnp.minimum(sizes[giver] - 1, reach - sizes[taker]) // 2
    margin = jnp.where((giver == sequence[0]) | (taker == sequence[0]) | (sizes[taker] == 0), 0, jnp.maximum(margin, 0))
    passed = jax.random.randint(jax.random.fold_in(own, 4), (amount // 2,), 0, 1 << 20) % (margin + 1)
    sizes = sizes.at[giver].add(-passed).at[taker].add(passed)
    labels = jnp.searchsorted(jnp.cumsum(sizes), jnp.arange(rows * top), side="right").astype(jnp.int32)
    grid = labels.reshape(top, rows).T
    grid = grid[jax.random.permutation(jax.random.fold_in(own, 1), rows)]
    rotation = jax.random.randint(jax.random.fold_in(own, 2), (rows, 1), 0, top)
    return jnp.take_along_axis(grid, (jnp.arange(top)[None, :] + rotation) % top, axis=1)


def shares(count, total, bound, skew, full):
    loads = [(1 << 20) // math.isqrt(grade ** skew) + 1 for grade in range(1, count + 1)]
    largest = bound if full else min(bound, max(-(-total // count), total * loads[0] // sum(loads)))
    least = 1 if total - largest >= count - 1 else 0
    counts, rest = [largest] + [least] * (count - 1), total - largest - least * (count - 1)
    while rest > 0:
        candidates = [i for i in range(1, count) if counts[i] < largest] or [i for i in range(1, count) if counts[i] < bound]
        mass, remaining = sum([loads[i] for i in candidates]), rest
        for i in candidates:
            addition = min(bound - counts[i], max(1, remaining * loads[i] // mass), rest)
            counts[i] = counts[i] + addition
            rest = rest - addition
    return np.array(counts)


def noise(own_key, dims, deviation, bound, cuts=(), kind=jnp.bfloat16):
    entries = jax.random.normal(own_key, dims, jnp.float32) * deviation
    if len(cuts) > 0:
        entries = steps_of(own_key, dims, cuts, -0.22, 0.18) * entries
    return jnp.clip(entries, min=-bound, max=bound).astype(kind)


def setup_inputs(seed: int = 0) -> dict:
    seeds = jax.random.split(jax.random.key(seed), 10)
    hidden_in = noise(seeds[0], (TOTAL_TOKENS, MODEL_WIDTH), 1.0, 6.0, ((0, 8), (1, 2)), jnp.float32)
    cotangent = noise(seeds[1], (TOTAL_TOKENS, MODEL_WIDTH), 1.0, 6.0, ((0, 8), (1, 2)), jnp.float32)
    norm_gains = jnp.clip(1.0 + 0.18 * jax.random.normal(seeds[2], (LAYER_COUNT, 2, MODEL_WIDTH), jnp.float32), 0.1, 1.9)
    query_key_value_weight = noise(seeds[3], (LAYER_COUNT, MODEL_WIDTH, (QUERY_HEADS + 2 * KEY_VALUE_HEADS) * HEAD_SIZE), MODEL_WIDTH ** -0.5, 0.1875, ((1, 2), (2, 8)))
    w_out = noise(seeds[4], (LAYER_COUNT, QUERY_HEADS * HEAD_SIZE, MODEL_WIDTH), HEAD_SIZE ** -0.5, 0.75, ((1, 8), (2, 2)))
    w_router = noise(seeds[5], (LAYER_COUNT, MODEL_WIDTH, E), MODEL_WIDTH ** -0.5, 0.1875, ((1, 2), (2, 8)))
    w_gate_up = noise(seeds[6], (LAYER_COUNT, E, MODEL_WIDTH, 2 * FF), MODEL_WIDTH ** -0.5, 0.1875, ((1, 8), (2, 2)))
    w_down = noise(seeds[7], (LAYER_COUNT, E, FF, MODEL_WIDTH), (FF // 8) ** -0.5, 0.75, ((1, 8), (3, 2)))
    expert_ids_keys = jax.random.split(jax.random.fold_in(seeds[8], 1), LAYER_COUNT * TOTAL_TOKENS // TOK_DEV)
    expert_ids_turns = jax.random.permutation(jax.random.fold_in(seeds[8], 3), LAYER_COUNT * TOTAL_TOKENS // TOK_DEV)
    expert_ids = jax.vmap(lambda own, number: deal_out(jax.random.fold_in(seeds[8], 2), own, number, TOK_DEV, E, TOP, CAP, 2))(expert_ids_keys, expert_ids_turns).reshape((LAYER_COUNT, TOTAL_TOKENS, TOP))
    return dict(hidden_in=hidden_in, cotangent=cotangent, norm_gains=norm_gains, query_key_value_weight=query_key_value_weight, w_out=w_out, w_router=w_router, w_gate_up=w_gate_up, w_down=w_down, expert_ids=expert_ids)


NORM_EPS = 1e-06
ROPE_BASE = 10000.0

def widen(value):
    return lax.optimization_barrier(value).astype(jnp.float32)

def rope_tables(seq_len, head_width):
    half_width = head_width // 2
    frequency = ROPE_BASE ** (-2.0 * jnp.arange(half_width, dtype=jnp.float32) / head_width)
    angles = jnp.arange(seq_len, dtype=jnp.float32)[:, None] * frequency[None, :]
    cosine = jnp.concatenate([jnp.cos(angles), jnp.cos(angles)], axis=1)
    sine_table = jnp.concatenate([jnp.sin(angles), jnp.sin(angles)], axis=1)
    return (cosine, sine_table)

def rotate(vector, cosine, sine_table):
    half_width = vector.shape[-1] // 2
    swapped = jnp.concatenate([-vector[..., half_width:], vector[..., :half_width]], axis=-1)
    return vector * cosine + swapped * sine_table

def rotate_back(gradient, cosine, sine_table):
    scaled = gradient * sine_table
    half_width = gradient.shape[-1] // 2
    swapped = jnp.concatenate([scaled[..., half_width:], -scaled[..., :half_width]], axis=-1)
    return gradient * cosine + swapped

def causal_mask(length):
    return lax.broadcasted_iota(jnp.int32, (length, length), 0) >= lax.broadcasted_iota(jnp.int32, (length, length), 1)

def attend_one(operands):
    queries, key_heads, value_heads = operands
    scores = jnp.einsum('sjgd,tjd->jgst', widen(queries), widen(key_heads)) * (1.0 / HEAD_SIZE)
    allowed = causal_mask(SEQUENCE_TOKENS)
    exponent = jnp.where(allowed, jnp.exp(scores), 0.0)
    log_total = jnp.log(lax.optimization_barrier(jnp.sum(exponent, axis=-1)))
    attn_probs = jnp.where(allowed, jnp.exp(scores - log_total[..., None]), 0.0).astype(jnp.bfloat16)
    attended = jnp.einsum('jgst,tjd->sjgd', widen(attn_probs), widen(value_heads)).astype(jnp.bfloat16)
    return (attended, log_total)

def attend_back_one(operands):
    queries, key_heads, value_heads, attended, log_total, attention_gradient = operands
    scores = jnp.einsum('sjgd,tjd->jgst', widen(queries), widen(key_heads)) * (1.0 / HEAD_SIZE)
    allowed = causal_mask(SEQUENCE_TOKENS)
    attn_probs = jnp.where(allowed, jnp.exp(scores - log_total[..., None]), 0.0)
    probs_low = widen(attn_probs.astype(jnp.bfloat16))
    grad_wide = widen(attention_gradient)
    grad_values = jnp.einsum('jgst,sjgd->tjd', probs_low, grad_wide)
    grad_probs = jnp.einsum('sjgd,tjd->jgst', grad_wide, widen(value_heads))
    row_delta = jnp.einsum('sjgd,sjgd->jgs', grad_wide, widen(attended))
    grad_score = (attn_probs * (grad_probs - row_delta[..., None]) * (1.0 / HEAD_SIZE)).astype(jnp.bfloat16)
    score_wide = widen(grad_score)
    grad_queries = jnp.einsum('jgst,tjd->sjgd', score_wide, widen(key_heads))
    grad_keys = jnp.einsum('jgst,sjgd->tjd', score_wide, widen(queries))
    return (grad_queries, grad_keys, grad_values)

def norm_back(hidden, scaling, gain_row, grad_normed):
    weighted = grad_normed * gain_row
    inner = lax.optimization_barrier(jnp.sum(weighted * hidden, axis=1))
    grad_hidden = scaling[:, None] * weighted - hidden * (scaling ** 3 * inner / MODEL_WIDTH)[:, None]
    grad_gain = lax.optimization_barrier(jnp.sum(grad_normed * hidden * scaling[:, None], axis=0))
    return (grad_hidden, grad_gain)

def expert_slots(routes, gate_prob, expert):
    matches = routes == expert
    routed = jnp.any(matches, axis=1)
    weight = lax.optimization_barrier(jnp.sum(jnp.where(matches, gate_prob, 0.0), axis=1))
    rank_in = jnp.cumsum(routed.astype(jnp.int32)) - 1
    capacity = CAP * N_DP
    placed = jnp.where(routed, rank_in, capacity).astype(jnp.int32)
    token_ids = jnp.arange(routes.shape[0], dtype=jnp.int32)
    slot_tokens = jnp.zeros((capacity,), jnp.int32).at[placed].set(token_ids, mode='drop')
    slot_gate = jnp.zeros((capacity,), jnp.float32).at[placed].set(weight, mode='drop')
    slot_valid = jnp.arange(capacity, dtype=jnp.int32) < jnp.sum(routed.astype(jnp.int32))
    return (slot_tokens, slot_gate, slot_valid)

def expert_compute(normed_two, slot_tokens, gate_up, down_proj):
    slot_rows = normed_two[slot_tokens]
    pre_act = jnp.dot(slot_rows, gate_up, preferred_element_type=jnp.float32)
    activated = (jax.nn.silu(pre_act[:, :FF]) * pre_act[:, FF:]).astype(jnp.bfloat16)
    expert_out = jnp.dot(activated, down_proj, preferred_element_type=jnp.float32)
    return (slot_rows, pre_act, activated, expert_out)

def layer_forward(hidden, gain_pair, query_key_value_weight, w_out, w_router, w_gate_up, w_down, routes):
    cosine, sine_table = rope_tables(SEQUENCE_TOKENS, HEAD_SIZE)
    scale_one = lax.rsqrt(lax.optimization_barrier(jnp.mean(hidden * hidden, axis=1)) + NORM_EPS)
    normed_one = (hidden * scale_one[:, None] * gain_pair[0]).astype(jnp.bfloat16)
    query_key_value = jnp.dot(normed_one, query_key_value_weight, preferred_element_type=jnp.float32)
    head_grouped = query_key_value.reshape(TOTAL_TOKENS // SEQUENCE_TOKENS, SEQUENCE_TOKENS, KEY_VALUE_HEADS, QUERY_PER_GROUP + 2, HEAD_SIZE)
    queries = rotate(head_grouped[:, :, :, :QUERY_PER_GROUP], cosine[None, :, None, None, :], sine_table[None, :, None, None, :]).astype(jnp.bfloat16)
    key_heads = rotate(head_grouped[:, :, :, QUERY_PER_GROUP], cosine[None, :, None, :], sine_table[None, :, None, :]).astype(jnp.bfloat16)
    value_heads = head_grouped[:, :, :, QUERY_PER_GROUP + 1].astype(jnp.bfloat16)
    attended, log_total = lax.map(attend_one, (queries, key_heads, value_heads))
    attn_flat = attended.reshape(TOTAL_TOKENS, QUERY_HEADS * HEAD_SIZE)
    middle = hidden + jnp.dot(attn_flat, w_out, preferred_element_type=jnp.float32)
    scale_two = lax.rsqrt(lax.optimization_barrier(jnp.mean(middle * middle, axis=1)) + NORM_EPS)
    normed_two = (middle * scale_two[:, None] * gain_pair[1]).astype(jnp.bfloat16)
    logits = jnp.dot(normed_two, w_router, preferred_element_type=jnp.float32)
    chosen = jnp.take_along_axis(logits, routes, axis=1)
    exponent = jnp.exp(chosen)
    gate_prob = exponent / lax.optimization_barrier(jnp.sum(exponent, axis=1, keepdims=True))

    def expert_step(moe_sum, operands):
        gate_up, down_proj, expert = operands
        slot_tokens, slot_gate, slot_valid = expert_slots(routes, gate_prob, expert)
        slot_rows, pre_act, activated, expert_out = expert_compute(normed_two, slot_tokens, gate_up, down_proj)
        return (moe_sum.at[slot_tokens].add(slot_gate[:, None] * expert_out), None)
    moe_sum, unused = lax.scan(expert_step, jnp.zeros((TOTAL_TOKENS, MODEL_WIDTH), jnp.float32), (w_gate_up, w_down, jnp.arange(E, dtype=jnp.int32)))
    result = middle + moe_sum
    record = {'hidden': hidden, 'scale_one': scale_one, 'normed_one': normed_one, 'queries': queries, 'key_heads': key_heads, 'value_heads': value_heads, 'attended': attended, 'log_total': log_total, 'attn_flat': attn_flat, 'middle': middle, 'scale_two': scale_two, 'normed_two': normed_two, 'gate_prob': gate_prob}
    return (result, record)

def layer_backward(record, gain_pair, query_key_value_weight, w_out, w_router, w_gate_up, w_down, routes, grad_result):
    cosine, sine_table = rope_tables(SEQUENCE_TOKENS, HEAD_SIZE)
    normed_two = record['normed_two']
    gate_prob = record['gate_prob']

    def expert_back(grad_rows, operands):
        gate_up, down_proj, expert = operands
        slot_tokens, slot_gate, slot_valid = expert_slots(routes, gate_prob, expert)
        slot_rows, pre_act, activated, expert_out = expert_compute(normed_two, slot_tokens, gate_up, down_proj)
        upstream = grad_result[slot_tokens]
        grad_expert = (slot_gate[:, None] * upstream).astype(jnp.bfloat16)
        grad_wdown = jnp.dot(activated.T, grad_expert, preferred_element_type=jnp.float32)
        back_grad = jnp.dot(grad_expert, down_proj.T, preferred_element_type=jnp.float32)
        gate_part = pre_act[:, :FF]
        up_part = pre_act[:, FF:]
        sigmoid_v = jax.nn.sigmoid(gate_part)
        grad_pre = jnp.concatenate([back_grad * up_part * sigmoid_v * (1.0 + gate_part * (1.0 - sigmoid_v)), back_grad * gate_part * sigmoid_v], axis=1).astype(jnp.bfloat16)
        grad_wgu = jnp.dot(slot_rows.T, grad_pre, preferred_element_type=jnp.float32)
        grad_rows = grad_rows.at[slot_tokens].add(jnp.dot(grad_pre, gate_up.T, preferred_element_type=jnp.float32))
        row_dot = jnp.where(slot_valid, lax.optimization_barrier(jnp.sum(upstream * expert_out, axis=1)), 0.0)
        gate_column = jnp.zeros((TOTAL_TOKENS,), jnp.float32).at[slot_tokens].add(row_dot)
        return (grad_rows, (grad_wgu, grad_wdown, gate_column))
    grad_rows, (grad_gate_up, grad_down, gate_columns) = lax.scan(expert_back, jnp.zeros((TOTAL_TOKENS, MODEL_WIDTH), jnp.float32), (w_gate_up, w_down, jnp.arange(E, dtype=jnp.int32)))
    grad_gate = jnp.take_along_axis(gate_columns.T, routes, axis=1)
    mean_term = lax.optimization_barrier(jnp.sum(gate_prob * grad_gate, axis=1, keepdims=True))
    grad_chosen = gate_prob * (grad_gate - mean_term)
    token_rows = jnp.arange(TOTAL_TOKENS, dtype=jnp.int32)[:, None]
    grad_logit = jnp.zeros((TOTAL_TOKENS, E), jnp.float32).at[token_rows, routes].add(grad_chosen).astype(jnp.bfloat16)
    grad_router = jnp.dot(normed_two.T, grad_logit, preferred_element_type=jnp.float32)
    grad_normed = grad_rows + jnp.dot(grad_logit, w_router.T, preferred_element_type=jnp.float32)
    grad_middle, gain_two = norm_back(record['middle'], record['scale_two'], gain_pair[1], grad_normed)
    grad_middle = grad_middle + grad_result
    grad_mid_low = grad_middle.astype(jnp.bfloat16)
    grad_out = jnp.dot(record['attn_flat'].T, grad_mid_low, preferred_element_type=jnp.float32)
    attention_gradient = jnp.dot(grad_mid_low, w_out.T, preferred_element_type=jnp.float32).astype(jnp.bfloat16)
    attention_gradient = attention_gradient.reshape(TOTAL_TOKENS // SEQUENCE_TOKENS, SEQUENCE_TOKENS, KEY_VALUE_HEADS, QUERY_PER_GROUP, HEAD_SIZE)
    grad_queries, grad_keys, grad_values = lax.map(attend_back_one, (record['queries'], record['key_heads'], record['value_heads'], record['attended'], record['log_total'], attention_gradient))
    grad_queries = rotate_back(grad_queries, cosine[None, :, None, None, :], sine_table[None, :, None, None, :])
    grad_keys = rotate_back(grad_keys, cosine[None, :, None, :], sine_table[None, :, None, :])
    column_gradient = jnp.concatenate([grad_queries, grad_keys[:, :, :, None], grad_values[:, :, :, None]], axis=3)
    column_gradient = column_gradient.reshape(TOTAL_TOKENS, (QUERY_HEADS + 2 * KEY_VALUE_HEADS) * HEAD_SIZE).astype(jnp.bfloat16)
    grad_qkv = jnp.dot(record['normed_one'].T, column_gradient, preferred_element_type=jnp.float32)
    grad_normed_one = jnp.dot(column_gradient, query_key_value_weight.T, preferred_element_type=jnp.float32)
    grad_hidden, gain_one = norm_back(record['hidden'], record['scale_one'], gain_pair[0], grad_normed_one)
    grad_hidden = grad_hidden + grad_middle
    grad_gains = jnp.stack([gain_one, gain_two])
    return (grad_hidden, (grad_gains, grad_qkv, grad_out, grad_router, grad_gate_up, grad_down))

def reference(hidden_in, cotangent, norm_gains, query_key_value_weight, w_out, w_router, w_gate_up, w_down, expert_ids):
    layers = query_key_value_weight.shape[0]
    records = []
    current = hidden_in
    for layer_index in range(layers):
        current, record = layer_forward(current, norm_gains[layer_index], query_key_value_weight[layer_index], w_out[layer_index], w_router[layer_index], w_gate_up[layer_index], w_down[layer_index], expert_ids[layer_index])
        records.append(record)
    grad_current = cotangent
    collected = [None] * layers
    for layer_index in reversed(range(layers)):
        grad_current, grads = layer_backward(records[layer_index], norm_gains[layer_index], query_key_value_weight[layer_index], w_out[layer_index], w_router[layer_index], w_gate_up[layer_index], w_down[layer_index], expert_ids[layer_index], grad_current)
        collected[layer_index] = grads
    stacks = [jnp.stack([collected[layer_index][member] for layer_index in range(layers)]) for member in range(6)]
    return (current, grad_current, stacks[0], stacks[1], stacks[2], stacks[3], stacks[4], stacks[5])
```

```python
import jax
import jax.numpy as jnp
from jax import lax
from jax.sharding import PartitionSpec as P

MODEL_WIDTH = 1024
HALF = 512
HEAD_SIZE = 64
FF = 512
TOKENS = 256
PEERS = 16
OWN_TOKENS = 16
N_DP = 8
NORM_EPS = 1e-06
ROPE_BASE = 10000.0
GROUP = ("row", "col")
F32 = jnp.float32
BF16 = jnp.bfloat16


def dot(a, b, dims):
    return lax.dot_general(a, b, (dims, ((), ())), preferred_element_type=F32)


def mm(a, b):
    return dot(a, b, ((1,), (0,)))


def mm_nt(a, b):
    return dot(a, b, ((1,), (1,)))


def mm_tn(a, b):
    return dot(a, b, ((0,), (0,)))


def row_swap(value):
    return lax.ppermute(value, "row", [(0, 1), (1, 0)])


def swap_halves(value):
    return jnp.concatenate([value[..., HALF:MODEL_WIDTH], value[..., :HALF]], axis=-1)


def split_two(value):
    high = lax.reduce_precision(value, 8, 7)
    return (high.astype(BF16), (value - high).astype(BF16))


def rope_tables():
    half_width = HEAD_SIZE // 2
    frequency = ROPE_BASE ** (-2.0 * jnp.arange(half_width, dtype=F32) / HEAD_SIZE)
    angles = jnp.arange(TOKENS, dtype=F32)[:, None] * frequency[None, :]
    cosine = jnp.concatenate([jnp.cos(angles), jnp.cos(angles)], axis=1)
    sine = jnp.concatenate([jnp.sin(angles), jnp.sin(angles)], axis=1)
    return (cosine, sine)


def rotate(vector, cosine, sine):
    half = HEAD_SIZE // 2
    swapped = jnp.concatenate([-vector[:, half:], vector[:, :half]], axis=1)
    return vector * cosine + swapped * sine


def rotate_back(gradient, cosine, sine):
    half = HEAD_SIZE // 2
    scaled = gradient * sine
    swapped = jnp.concatenate([scaled[:, half:], -scaled[:, :half]], axis=1)
    return gradient * cosine + swapped


def causal():
    return lax.broadcasted_iota(jnp.int32, (TOKENS, TOKENS), 0) >= lax.broadcasted_iota(
        jnp.int32, (TOKENS, TOKENS), 1
    )


def reduce_tokens(partial, extra=None):
    chunks = partial.reshape(PEERS, OWN_TOKENS, MODEL_WIDTH)
    if extra is not None:
        chunks = jnp.concatenate(
            [chunks, jnp.broadcast_to(extra[None], (PEERS,) + extra.shape)], axis=2
        )
    got = lax.all_to_all(chunks, GROUP, 0, 0, tiled=True).astype(F32)
    first = jnp.sum(got[:8, :, :MODEL_WIDTH], axis=0)
    second = jnp.sum(got[8:, :, :MODEL_WIDTH], axis=0)
    total = first + swap_halves(second)
    if extra is None:
        return total
    return (total, jnp.sum(got[:, :, MODEL_WIDTH:], axis=0))


def gather_tokens(rows, extra=None):
    swapped = swap_halves(rows)
    if extra is not None:
        rows = jnp.concatenate([rows, extra], axis=1)
        swapped = jnp.concatenate([swapped, extra], axis=1)
    width = rows.shape[1]
    send = jnp.concatenate(
        [
            jnp.broadcast_to(rows[None], (8, OWN_TOKENS, width)),
            jnp.broadcast_to(swapped[None], (8, OWN_TOKENS, width)),
        ]
    )
    got = lax.all_to_all(send, GROUP, 0, 0, tiled=True)
    full = got[:, :, :MODEL_WIDTH].reshape(TOKENS, MODEL_WIDTH)
    if extra is None:
        return full
    return (full, got[:, :, MODEL_WIDTH:])


def pack_vector(vector):
    high, low = split_two(vector)
    return jnp.concatenate([high.reshape(8, 128), low.reshape(8, 128)])


def unpack_vector(packed):
    return (packed[:8] + packed[8:]).reshape(MODEL_WIDTH)


def norm_forward(hidden, gain):
    scaling = lax.rsqrt(jnp.mean(hidden * hidden, axis=1, keepdims=True) + NORM_EPS)
    return (scaling, (hidden * scaling * gain).astype(BF16))


def norm_back(hidden, scaling, gain, grad_normed):
    weighted = grad_normed * gain
    inner = jnp.sum(weighted * hidden, axis=1, keepdims=True)
    return scaling * weighted - hidden * (scaling**3 * inner / MODEL_WIDTH)


def attention_forward(normed, w_heads, w_out, cosine, sine):
    qkv = mm(normed, w_heads)
    query = rotate(qkv[:, :HEAD_SIZE], cosine, sine).astype(BF16)
    key = rotate(qkv[:, HEAD_SIZE : 2 * HEAD_SIZE], cosine, sine).astype(BF16)
    value = qkv[:, 2 * HEAD_SIZE :].astype(BF16)
    scores = mm_nt(query, key) * (1.0 / HEAD_SIZE)
    allowed = causal()
    total = jnp.log(jnp.sum(jnp.where(allowed, jnp.exp(scores), 0.0), axis=1, keepdims=True))
    probs = jnp.where(allowed, jnp.exp(scores - total), 0.0).astype(BF16)
    attended = mm(probs, value).astype(BF16)
    partial = mm(attended, w_out).astype(BF16)
    return (partial, (query, key, value, attended, total))


def attention_back(saved, normed, grad_low, w_heads, w_out, cosine, sine):
    query, key, value, attended, total = saved
    grad_attended = mm_nt(grad_low, w_out).astype(BF16)
    grad_out = mm_tn(attended, grad_low)
    scores = mm_nt(query, key) * (1.0 / HEAD_SIZE)
    probs = jnp.where(causal(), jnp.exp(scores - total), 0.0)
    grad_value = mm_tn(probs.astype(BF16), grad_attended)
    grad_probs = mm_nt(grad_attended, value)
    delta = jnp.sum(grad_attended.astype(F32) * attended.astype(F32), axis=1, keepdims=True)
    grad_scores = (probs * (grad_probs - delta) * (1.0 / HEAD_SIZE)).astype(BF16)
    grad_query = rotate_back(mm(grad_scores, key), cosine, sine)
    grad_key = rotate_back(mm_tn(grad_scores, query), cosine, sine)
    columns = jnp.concatenate([grad_query, grad_key, grad_value], axis=1).astype(BF16)
    grad_heads = mm_tn(normed, columns)
    grad_normed = mm_nt(columns, w_heads).astype(BF16)
    return (grad_normed, grad_heads, grad_out)


def gates_of(normed, router, routes):
    logits = mm_nt(normed, router)
    experts = jnp.arange(logits.shape[1], dtype=jnp.int32)
    chosen = jnp.any(routes[:, :, None] == experts[None, None, :], axis=1)
    exponent = jnp.where(chosen, jnp.exp(logits), 0.0)
    return exponent / jnp.sum(exponent, axis=1, keepdims=True)


def experts_forward(normed, gates, up_own, up_other, down_own, down_other):
    pre = []
    partial = 0.0
    for e in range(2):
        pre_e = mm(normed[:, :HALF], up_own[e]) + mm(normed[:, HALF:], up_other[e])
        act = (jax.nn.silu(pre_e[:, :FF]) * pre_e[:, FF:]).astype(BF16)
        out_e = jnp.concatenate([mm(act, down_own[e]), mm(act, down_other[e])], axis=1)
        partial = partial + gates[e] * out_e
        pre.append(pre_e)
    return (partial.astype(BF16), pre)


def experts_back(normed, gates, pre, up_own, up_other, down_own, down_other, upstream, mean):
    grad_normed = 0.0
    grad_logits = []
    pieces = []
    downs = []
    for e in range(2):
        gate_part, up_part = pre[e][:, :FF], pre[e][:, FF:]
        sig = jax.nn.sigmoid(gate_part)
        act = (gate_part * sig * up_part).astype(BF16)
        raw = mm_nt(upstream[:, :HALF], down_own[e]) + mm_nt(upstream[:, HALF:], down_other[e])
        grad_gate = jnp.sum(act.astype(F32) * raw, axis=1, keepdims=True)
        back = gates[e] * raw
        grad_pre = jnp.concatenate(
            [back * up_part * sig * (1.0 + gate_part * (1.0 - sig)), back * gate_part * sig], axis=1
        ).astype(BF16)
        grad_y = (gates[e] * upstream.astype(F32)).astype(BF16)
        downs.append(mm_tn(act, grad_y).astype(BF16).reshape(N_DP, 64, MODEL_WIDTH))
        grad_up = mm_tn(normed, grad_pre).astype(BF16).reshape(2, N_DP, 64, MODEL_WIDTH)
        pieces.append(grad_up[0])
        pieces.append(grad_up[1])
        grad_normed = grad_normed + jnp.concatenate(
            [mm_nt(grad_pre, up_own[e]), mm_nt(grad_pre, up_other[e])], axis=1
        )
        grad_logits.append((gates[e] * (grad_gate - mean)).astype(BF16))
    pack = jnp.concatenate(pieces + downs, axis=1)
    return (grad_normed, grad_logits, pack)


def body(
    hidden_in,
    cotangent,
    norm_gains,
    query_key_value_weight,
    w_out,
    w_router,
    w_gate_up,
    w_down,
    expert_ids,
):
    r = lax.axis_index("row")
    c = lax.axis_index("col")
    lower = r == 0
    layers = 2

    def natural(own, other):
        return jnp.where(
            lower,
            jnp.concatenate([own, other], axis=-1),
            jnp.concatenate([other, own], axis=-1),
        )

    def own_first(vector):
        return jnp.where(lower, vector, swap_halves(vector))

    cosine, sine = rope_tables()

    gain_first = norm_gains[0, 0]
    square = jnp.sum(hidden_in * hidden_in, axis=1, keepdims=True)
    high, low = split_two(square)
    sent = jnp.concatenate(
        [
            (hidden_in * gain_first).astype(BF16),
            high,
            low,
            jnp.zeros((TOKENS, 126), BF16),
        ],
        axis=1,
    )
    got = row_swap(sent)
    square = square + got[:, HALF : HALF + 1].astype(F32) + got[:, HALF + 1 : HALF + 2].astype(F32)
    scale_all = lax.rsqrt(square / MODEL_WIDTH + NORM_EPS)
    normed_first = jnp.concatenate(
        [hidden_in * scale_all * gain_first, got[:, :HALF].astype(F32) * scale_all], axis=1
    ).astype(BF16)

    q_low = query_key_value_weight[:, :, :HEAD_SIZE]
    q_high = query_key_value_weight[:, :, HEAD_SIZE : 2 * HEAD_SIZE]
    kv = query_key_value_weight[:, :, 2 * HEAD_SIZE :]
    heads_own = jnp.concatenate([jnp.where(lower, q_low, q_high), kv], axis=2)
    heads_sent = jnp.concatenate([jnp.where(lower, q_high, q_low), kv], axis=2)
    heads = jnp.concatenate([heads_own, row_swap(heads_sent)], axis=1)
    out_low, out_high = w_out[:, :HEAD_SIZE], w_out[:, HEAD_SIZE:]
    out_rows = jnp.concatenate(
        [jnp.where(lower, out_low, out_high), row_swap(jnp.where(lower, out_high, out_low))], axis=2
    )

    mine = (r * 8 + c) * OWN_TOKENS
    theirs = ((1 - r) * 8 + c) * OWN_TOKENS
    gains_flat = norm_gains.reshape(4, HALF)
    small = jnp.concatenate(
        [
            lax.dynamic_slice(hidden_in, (theirs, 0), (OWN_TOKENS, HALF)),
            lax.dynamic_slice(cotangent, (theirs, 0), (OWN_TOKENS, HALF)),
            gains_flat,
            jnp.zeros((4, HALF), F32),
        ]
    )
    small = row_swap(small)
    hidden = natural(
        lax.dynamic_slice(hidden_in, (mine, 0), (OWN_TOKENS, HALF)), small[:OWN_TOKENS]
    )
    grad_tokens = natural(
        lax.dynamic_slice(cotangent, (mine, 0), (OWN_TOKENS, HALF)),
        small[OWN_TOKENS : 2 * OWN_TOKENS],
    )
    gains = natural(gains_flat, small[2 * OWN_TOKENS : 2 * OWN_TOKENS + 4])

    ups, downs = [], []
    for layer in range(layers):
        up_own = lax.dynamic_slice(w_gate_up[layer], (2 * r, 0, 0), (2, HALF, 2 * FF))
        up_sent = lax.dynamic_slice(w_gate_up[layer], (2 - 2 * r, 0, 0), (2, HALF, 2 * FF))
        down_own = lax.dynamic_slice(w_down[layer], (2 * r, 0, 0), (2, FF, HALF))
        down_sent = lax.dynamic_slice(w_down[layer], (2 - 2 * r, 0, 0), (2, FF, HALF))
        ups.append((up_own, row_swap(up_sent)))
        downs.append((down_own, row_swap(down_sent)))
    cot_low = cotangent.astype(BF16)
    upstream = jnp.concatenate([cot_low, row_swap(cot_low)], axis=1)

    router_rows = jnp.transpose(w_router, (2, 0, 1)).reshape(OWN_TOKENS, 256)

    first_expert = 4 * c + 2 * r
    expert_range = jnp.arange(32, dtype=jnp.int32)[None, :]
    routers = None
    records = []
    normed = normed_first
    scale_one = None
    for layer in range(layers):
        partial, saved = attention_forward(normed, heads[layer], out_rows[layer], cosine, sine)
        middle = hidden + reduce_tokens(partial)
        scale_two, rows = norm_forward(middle, gains[2 * layer + 1])
        if layer == 0:
            normed_two, extra = gather_tokens(rows, router_rows)
            table = extra.reshape(2, 8, OWN_TOKENS, 256).reshape(2, 32, 2, HALF)
            table = jnp.where(lower, table, table[::-1])
            routers = [
                jnp.concatenate([table[0, :, i], table[1, :, i]], axis=1) for i in range(layers)
            ]
        else:
            normed_two = gather_tokens(rows)
        all_gates = gates_of(normed_two, routers[layer], expert_ids[layer])
        gates = [
            jnp.sum(jnp.where(expert_range == first_expert + e, all_gates, 0.0), 1, keepdims=True)
            for e in range(2)
        ]
        partial, pre = experts_forward(normed_two, gates, *ups[layer], *downs[layer])
        mixed = reduce_tokens(partial)
        result = middle + mixed
        records.append(
            dict(
                hidden=hidden,
                scale_one=scale_one,
                normed_one=normed,
                saved=saved,
                middle=middle,
                scale_two=scale_two,
                normed_two=normed_two,
                gates=gates,
                pre=pre,
                mixed=mixed,
            )
        )
        hidden = result
        if layer + 1 < layers:
            scale_one, rows = norm_forward(result, gains[2 * layer + 2])
            normed = gather_tokens(rows)

    def mean_columns(grad_rows, mixed_rows):
        high, low = split_two(jnp.sum(grad_rows * mixed_rows, axis=1, keepdims=True))
        return jnp.concatenate([high, low, jnp.zeros((OWN_TOKENS, 126), BF16)], axis=1)

    def mean_of(extra):
        flat = extra.reshape(TOKENS, 128).astype(F32)
        return flat[:, :1] + flat[:, 1:2]

    def spread_halves(rows, extra=None):
        low_half, high_half = rows[:, :HALF].astype(BF16), rows[:, HALF:].astype(BF16)
        if extra is not None:
            low_half = jnp.concatenate([low_half, extra], axis=1)
            high_half = jnp.concatenate([high_half, extra], axis=1)
        width = low_half.shape[1]
        send = jnp.concatenate(
            [
                jnp.broadcast_to(low_half[None], (8, OWN_TOKENS, width)),
                jnp.broadcast_to(high_half[None], (8, OWN_TOKENS, width)),
            ]
        )
        got = lax.all_to_all(send, GROUP, 0, 0, tiled=True)
        return got.reshape(TOKENS, width)

    got = spread_halves(hidden, mean_columns(grad_tokens, records[-1]["mixed"]))
    block_out = got[:, :HALF].astype(F32)
    mean = mean_of(got[:, HALF:])

    packs, smalls = [None] * layers, [None] * layers
    gain_sums = [None] * 4
    for layer in reversed(range(layers)):
        rec = records[layer]
        grad_normed, grad_logits, pack = experts_back(
            rec["normed_two"], rec["gates"], rec["pre"], *ups[layer], *downs[layer], upstream, mean
        )
        packs[layer] = lax.psum_scatter(pack, "dp", scatter_dimension=0, tiled=True)
        dense = jnp.zeros((TOKENS, 32), F32)
        for e in range(2):
            dense = jnp.where(expert_range == first_expert + e, grad_logits[e].astype(F32), dense)
        grad_normed = grad_normed + mm(dense.astype(BF16), routers[layer])
        local_ids = 4 * c + jnp.arange(4, dtype=jnp.int32)[None, :]
        local = jnp.zeros((TOKENS, 4), F32)
        for e in range(2):
            local = jnp.where(local_ids == first_expert + e, grad_logits[e].astype(F32), local)
        grad_router = mm_tn(rec["normed_two"], local.astype(BF16))
        total = reduce_tokens(grad_normed.astype(BF16))
        gain_two = gains[2 * layer + 1]
        grad_middle = grad_tokens + norm_back(rec["middle"], rec["scale_two"], gain_two, total)
        gain_part = jnp.sum(total * rec["middle"] * rec["scale_two"], axis=0)
        grad_low, extra = gather_tokens(grad_middle.astype(BF16), pack_vector(gain_part))
        gain_sums[2 * layer + 1] = unpack_vector(jnp.sum(extra.astype(F32), axis=0))
        grad_normed, grad_heads, grad_out = attention_back(
            rec["saved"], rec["normed_one"], grad_low, heads[layer], out_rows[layer], cosine, sine
        )
        gain_one = gains[2 * layer]
        gain_part = jnp.sum(grad_heads * heads[layer].astype(F32), axis=1)
        gain_part = own_first(gain_part) / gain_one
        total, extra = reduce_tokens(grad_normed, pack_vector(gain_part))
        gain_sums[2 * layer] = unpack_vector(extra)
        scale_one = rec["scale_one"]
        if layer == 0:
            scale_one = lax.rsqrt(
                jnp.mean(rec["hidden"] * rec["hidden"], axis=1, keepdims=True) + NORM_EPS
            )
        grad_tokens = grad_middle + norm_back(rec["hidden"], scale_one, gain_one, total)
        if layer > 0:
            upstream, extra = gather_tokens(
                grad_tokens.astype(BF16), mean_columns(grad_tokens, records[layer - 1]["mixed"])
            )
            mean = mean_of(extra)
        zero = jnp.zeros((MODEL_WIDTH, HEAD_SIZE), F32)
        q_grad = grad_heads[:, :HEAD_SIZE]
        q_wide = jnp.where(
            lower,
            jnp.concatenate([q_grad, zero], axis=1),
            jnp.concatenate([zero, q_grad], axis=1),
        )
        head_part = jnp.concatenate([q_wide, grad_heads[:, HEAD_SIZE:]], axis=1)
        head_part = head_part.reshape(2, N_DP, 64, 256)
        gain_cols = jnp.zeros((MODEL_WIDTH, 4), F32)
        if layer == 0:
            gain_cols = jnp.stack([0.5 * own_first(g) for g in gain_sums], axis=1)
        tail_part = jnp.concatenate(
            [grad_router, gain_cols, jnp.zeros((MODEL_WIDTH, 120), F32)], axis=1
        ).reshape(2, N_DP, 64, 128)
        zero = jnp.zeros_like(grad_out)
        out_part = jnp.where(
            lower,
            jnp.concatenate([grad_out, zero], axis=0),
            jnp.concatenate([zero, grad_out], axis=0),
        )
        out_part = out_part.reshape(N_DP, 16, 2, 4, 128).transpose(2, 0, 3, 1, 4)
        out_part = out_part.reshape(2, N_DP, 64, 128)
        part = jnp.concatenate([head_part, out_part, tail_part], axis=3).astype(BF16)
        smalls[layer] = part.transpose(1, 0, 2, 3)

    got = spread_halves(grad_tokens)
    grad_hidden = got.astype(F32)

    grads = []
    for layer in range(layers):
        if layer == 0:
            got = lax.all_to_all(
                smalls[layer].reshape(N_DP, 128, 512), "dp", 0, 0, tiled=True
            ).astype(F32)
            mine_small = jnp.sum(got, axis=0)
        else:
            mine_small = lax.psum_scatter(
                smalls[layer].reshape(N_DP, 128, 512), "dp", scatter_dimension=0, tiled=True
            ).astype(F32)[0]
        big = packs[layer][0]
        sent = jnp.concatenate([mine_small[64:].astype(BF16)], axis=0)
        total = mine_small[:64] + row_swap(sent).astype(F32)
        grad_qkv = total[:, :256]
        grad_out = total[:, 256:384].reshape(4, 16, 128).transpose(1, 0, 2).reshape(16, HALF)
        grad_router = total[:, 384:388]
        gain_grad = total[:, 388:392]
        up_pieces = big[:256].reshape(2, 2, 64, MODEL_WIDTH)
        down_pieces = big[256:].reshape(2, 64, MODEL_WIDTH)
        up_other = row_swap(up_pieces[:, 1])
        down_other = row_swap(down_pieces[:, :, HALF:])
        up_mine, down_mine = up_pieces[:, 0], down_pieces[:, :, :HALF]
        grad_up = jnp.where(
            lower,
            jnp.concatenate([up_mine, up_other]),
            jnp.concatenate([up_other, up_mine]),
        ).astype(F32)
        grad_down = jnp.where(
            lower,
            jnp.concatenate([down_mine, down_other]),
            jnp.concatenate([down_other, down_mine]),
        ).astype(F32)
        grads.append((gain_grad, grad_qkv, grad_out, grad_router, grad_up, grad_down))
    gain_out = grads[0][0].T.reshape(2, 2, 64)
    return (block_out, grad_hidden, gain_out) + tuple(
        jnp.stack([grads[layer][i] for layer in range(layers)]) for i in range(1, 6)
    )


def solution(mesh):
    placed = (
        P("dp", "row"),
        P("dp", "row"),
        P(None, None, "row"),
        P(None, "row", "col"),
        P(None, "col", "row"),
        P(None, "row", "col"),
        P(None, "col", "row", None),
        P(None, "col", None, "row"),
        P(None, "dp", None),
    )
    return jax.shard_map(
        body,
        mesh=mesh,
        in_specs=placed,
        out_specs=(
            P("dp", "row"),
            P("dp", "row"),
            P(None, None, ("row", "dp")),
            P(None, ("row", "dp"), "col"),
            P(None, ("col", "dp"), "row"),
            P(None, ("row", "dp"), "col"),
            P(None, "col", ("row", "dp"), None),
            P(None, "col", "dp", "row"),
        ),
        check_vma=False,
    )
```

```python
import jax
import jax.numpy as jnp
from jax import lax
from jax.sharding import PartitionSpec as P

MODEL_WIDTH = 1024
HALF = 512
HEAD_SIZE = 64
FF = 512
TOKENS = 256
PEERS = 16
OWN_TOKENS = 16
N_DP = 8
NORM_EPS = 1e-06
ROPE_BASE = 10000.0
GROUP = ("row", "col")
F32 = jnp.float32
BF16 = jnp.bfloat16


def dot(a, b, dims):
    return lax.dot_general(a, b, (dims, ((), ())), preferred_element_type=F32)


def mm(a, b):
    return dot(a, b, ((1,), (0,)))


def mm_nt(a, b):
    return dot(a, b, ((1,), (1,)))


def mm_tn(a, b):
    return dot(a, b, ((0,), (0,)))


def row_swap(value):
    return lax.ppermute(value, "row", [(0, 1), (1, 0)])


def swap_halves(value):
    return jnp.concatenate([value[..., HALF:MODEL_WIDTH], value[..., :HALF]], axis=-1)


def split_two(value):
    high = lax.reduce_precision(value, 8, 7)
    return (high.astype(BF16), (value - high).astype(BF16))


def rope_tables():
    half_width = HEAD_SIZE // 2
    frequency = ROPE_BASE ** (-2.0 * jnp.arange(half_width, dtype=F32) / HEAD_SIZE)
    angles = jnp.arange(TOKENS, dtype=F32)[:, None] * frequency[None, :]
    cosine = jnp.concatenate([jnp.cos(angles), jnp.cos(angles)], axis=1)
    sine = jnp.concatenate([jnp.sin(angles), jnp.sin(angles)], axis=1)
    return (cosine, sine)


def rotate(vector, cosine, sine):
    half = HEAD_SIZE // 2
    swapped = jnp.concatenate([-vector[:, half:], vector[:, :half]], axis=1)
    return vector * cosine + swapped * sine


def rotate_back(gradient, cosine, sine):
    half = HEAD_SIZE // 2
    scaled = gradient * sine
    swapped = jnp.concatenate([scaled[:, half:], -scaled[:, :half]], axis=1)
    return gradient * cosine + swapped


def causal():
    return lax.broadcasted_iota(jnp.int32, (TOKENS, TOKENS), 0) >= lax.broadcasted_iota(
        jnp.int32, (TOKENS, TOKENS), 1
    )


def reduce_tokens(partial, extra=None):
    chunks = partial.reshape(PEERS, OWN_TOKENS, MODEL_WIDTH)
    if extra is not None:
        chunks = jnp.concatenate(
            [chunks, jnp.broadcast_to(extra[None], (PEERS,) + extra.shape)], axis=2
        )
    got = lax.all_to_all(chunks, GROUP, 0, 0, tiled=True).astype(F32)
    first = jnp.sum(got[:8, :, :MODEL_WIDTH], axis=0)
    second = jnp.sum(got[8:, :, :MODEL_WIDTH], axis=0)
    total = first + swap_halves(second)
    if extra is None:
        return total
    return (total, jnp.sum(got[:, :, MODEL_WIDTH:], axis=0))


def gather_tokens(rows, extra=None):
    swapped = swap_halves(rows)
    if extra is not None:
        rows = jnp.concatenate([rows, extra], axis=1)
        swapped = jnp.concatenate([swapped, extra], axis=1)
    width = rows.shape[1]
    send = jnp.concatenate(
        [
            jnp.broadcast_to(rows[None], (8, OWN_TOKENS, width)),
            jnp.broadcast_to(swapped[None], (8, OWN_TOKENS, width)),
        ]
    )
    got = lax.all_to_all(send, GROUP, 0, 0, tiled=True)
    full = got[:, :, :MODEL_WIDTH].reshape(TOKENS, MODEL_WIDTH)
    if extra is None:
        return full
    return (full, got[:, :, MODEL_WIDTH:])


def pack_vector(vector):
    high, low = split_two(vector)
    return jnp.concatenate([high.reshape(8, 128), low.reshape(8, 128)])


def unpack_vector(packed):
    return (packed[:8] + packed[8:]).reshape(MODEL_WIDTH)


def norm_forward(hidden, gain):
    scaling = lax.rsqrt(jnp.mean(hidden * hidden, axis=1, keepdims=True) + NORM_EPS)
    return (scaling, (hidden * scaling * gain).astype(BF16))


def norm_back(hidden, scaling, gain, grad_normed):
    weighted = grad_normed * gain
    inner = jnp.sum(weighted * hidden, axis=1, keepdims=True)
    return scaling * weighted - hidden * (scaling**3 * inner / MODEL_WIDTH)


def attention_forward(normed, w_heads, w_out, cosine, sine):
    qkv = mm(normed, w_heads)
    query = rotate(qkv[:, :HEAD_SIZE], cosine, sine).astype(BF16)
    key = rotate(qkv[:, HEAD_SIZE : 2 * HEAD_SIZE], cosine, sine).astype(BF16)
    value = qkv[:, 2 * HEAD_SIZE :].astype(BF16)
    scores = mm_nt(query, key) * (1.0 / HEAD_SIZE)
    allowed = causal()
    total = jnp.log(jnp.sum(jnp.where(allowed, jnp.exp(scores), 0.0), axis=1, keepdims=True))
    probs = jnp.where(allowed, jnp.exp(scores - total), 0.0).astype(BF16)
    attended = mm(probs, value).astype(BF16)
    partial = mm(attended, w_out).astype(BF16)
    return (partial, (query, key, value, attended, total))


def attention_back(saved, normed, grad_low, w_heads, w_out, cosine, sine):
    query, key, value, attended, total = saved
    grad_attended = mm_nt(grad_low, w_out).astype(BF16)
    grad_out = mm_tn(attended, grad_low)
    scores = mm_nt(query, key) * (1.0 / HEAD_SIZE)
    probs = jnp.where(causal(), jnp.exp(scores - total), 0.0)
    grad_value = mm_tn(probs.astype(BF16), grad_attended)
    grad_probs = mm_nt(grad_attended, value)
    delta = jnp.sum(grad_attended.astype(F32) * attended.astype(F32), axis=1, keepdims=True)
    grad_scores = (probs * (grad_probs - delta) * (1.0 / HEAD_SIZE)).astype(BF16)
    grad_query = rotate_back(mm(grad_scores, key), cosine, sine)
    grad_key = rotate_back(mm_tn(grad_scores, query), cosine, sine)
    columns = jnp.concatenate([grad_query, grad_key, grad_value], axis=1).astype(BF16)
    grad_heads = mm_tn(normed, columns)
    grad_normed = mm_nt(columns, w_heads).astype(BF16)
    return (grad_normed, grad_heads, grad_out)


def gates_of(normed, router, routes):
    logits = mm_nt(normed, router)
    experts = jnp.arange(logits.shape[1], dtype=jnp.int32)
    chosen = jnp.any(routes[:, :, None] == experts[None, None, :], axis=1)
    exponent = jnp.where(chosen, jnp.exp(logits), 0.0)
    return exponent / jnp.sum(exponent, axis=1, keepdims=True)


def experts_forward(normed, gates, up_own, up_other, down_own, down_other):
    pre = []
    partial = 0.0
    for e in range(2):
        pre_e = mm(normed[:, :HALF], up_own[e]) + mm(normed[:, HALF:], up_other[e])
        act = (jax.nn.silu(pre_e[:, :FF]) * pre_e[:, FF:]).astype(BF16)
        out_e = jnp.concatenate([mm(act, down_own[e]), mm(act, down_other[e])], axis=1)
        partial = partial + gates[e] * out_e
        pre.append(pre_e)
    return (partial.astype(BF16), pre)


def experts_back(normed, gates, pre, up_own, up_other, down_own, down_other, upstream, mean):
    grad_normed = 0.0
    grad_logits = []
    pieces = []
    downs = []
    for e in range(2):
        gate_part, up_part = pre[e][:, :FF], pre[e][:, FF:]
        sig = jax.nn.sigmoid(gate_part)
        act = (gate_part * sig * up_part).astype(BF16)
        raw = mm_nt(upstream[:, :HALF], down_own[e]) + mm_nt(upstream[:, HALF:], down_other[e])
        grad_gate = jnp.sum(act.astype(F32) * raw, axis=1, keepdims=True)
        back = gates[e] * raw
        grad_pre = jnp.concatenate(
            [back * up_part * sig * (1.0 + gate_part * (1.0 - sig)), back * gate_part * sig], axis=1
        ).astype(BF16)
        grad_y = (gates[e] * upstream.astype(F32)).astype(BF16)
        downs.append(mm_tn(act, grad_y).astype(BF16).reshape(N_DP, 64, MODEL_WIDTH))
        grad_up = mm_tn(normed, grad_pre).astype(BF16).reshape(2, N_DP, 64, MODEL_WIDTH)
        pieces.append(grad_up[0])
        pieces.append(grad_up[1])
        grad_normed = grad_normed + jnp.concatenate(
            [mm_nt(grad_pre, up_own[e]), mm_nt(grad_pre, up_other[e])], axis=1
        )
        grad_logits.append((gates[e] * (grad_gate - mean)).astype(BF16))
    pack = jnp.concatenate(pieces + downs, axis=1)
    return (grad_normed, grad_logits, pack)


def body(
    hidden_in,
    cotangent,
    norm_gains,
    query_key_value_weight,
    w_out,
    w_router,
    w_gate_up,
    w_down,
    expert_ids,
):
    r = lax.axis_index("row")
    c = lax.axis_index("col")
    lower = r == 0
    layers = 2

    def natural(own, other):
        return jnp.where(
            lower,
            jnp.concatenate([own, other], axis=-1),
            jnp.concatenate([other, own], axis=-1),
        )

    def own_first(vector):
        return jnp.where(lower, vector, swap_halves(vector))

    cosine, sine = rope_tables()

    gain_first = norm_gains[0, 0]
    square = jnp.sum(hidden_in * hidden_in, axis=1, keepdims=True)
    high, low = split_two(square)
    sent = jnp.concatenate(
        [
            (hidden_in * gain_first).astype(BF16),
            high,
            low,
            jnp.zeros((TOKENS, 126), BF16),
        ],
        axis=1,
    )
    got = row_swap(sent)
    square = square + got[:, HALF : HALF + 1].astype(F32) + got[:, HALF + 1 : HALF + 2].astype(F32)
    scale_all = lax.rsqrt(square / MODEL_WIDTH + NORM_EPS)
    normed_first = jnp.concatenate(
        [hidden_in * scale_all * gain_first, got[:, :HALF].astype(F32) * scale_all], axis=1
    ).astype(BF16)

    q_low = query_key_value_weight[:, :, :HEAD_SIZE]
    q_high = query_key_value_weight[:, :, HEAD_SIZE : 2 * HEAD_SIZE]
    kv = query_key_value_weight[:, :, 2 * HEAD_SIZE :]
    heads_own = jnp.concatenate([jnp.where(lower, q_low, q_high), kv], axis=2)
    heads_sent = jnp.concatenate([jnp.where(lower, q_high, q_low), kv], axis=2)
    heads = jnp.concatenate([heads_own, row_swap(heads_sent)], axis=1)
    out_low, out_high = w_out[:, :HEAD_SIZE], w_out[:, HEAD_SIZE:]
    out_rows = jnp.concatenate(
        [jnp.where(lower, out_low, out_high), row_swap(jnp.where(lower, out_high, out_low))], axis=2
    )

    mine = (r * 8 + c) * OWN_TOKENS
    theirs = ((1 - r) * 8 + c) * OWN_TOKENS
    gains_flat = norm_gains.reshape(4, HALF)
    small = jnp.concatenate(
        [
            lax.dynamic_slice(hidden_in, (theirs, 0), (OWN_TOKENS, HALF)),
            lax.dynamic_slice(cotangent, (theirs, 0), (OWN_TOKENS, HALF)),
            gains_flat,
            jnp.zeros((4, HALF), F32),
        ]
    )
    small = row_swap(small)
    hidden = natural(
        lax.dynamic_slice(hidden_in, (mine, 0), (OWN_TOKENS, HALF)), small[:OWN_TOKENS]
    )
    grad_tokens = natural(
        lax.dynamic_slice(cotangent, (mine, 0), (OWN_TOKENS, HALF)),
        small[OWN_TOKENS : 2 * OWN_TOKENS],
    )
    gains = natural(gains_flat, small[2 * OWN_TOKENS : 2 * OWN_TOKENS + 4])

    k = lax.axis_index("dp")
    ups, downs = [], []
    for layer in range(layers):
        up_own = lax.dynamic_slice(w_gate_up[layer], (2 * r, 0, 0), (2, HALF, 2 * FF))
        down_own = lax.dynamic_slice(w_down[layer], (2 * r, 0, 0), (2, FF, HALF))
        first_row = (2 - 2 * r) * HALF + 128 * k
        up_sent = lax.dynamic_slice(
            w_gate_up[layer].reshape(4 * HALF, 2 * FF), (first_row, 0), (128, 2 * FF)
        )
        down_sent = lax.dynamic_slice(
            w_down[layer].reshape(4 * FF, HALF), (first_row, 0), (128, HALF)
        )
        piece = row_swap(jnp.concatenate([up_sent, down_sent], axis=1))
        whole = lax.all_gather(piece, "dp", axis=0, tiled=True)
        ups.append((up_own, whole[:, : 2 * FF].reshape(2, HALF, 2 * FF)))
        downs.append((down_own, whole[:, 2 * FF :].reshape(2, FF, HALF)))
    cot_low = cotangent.astype(BF16)
    upstream = jnp.concatenate([cot_low, row_swap(cot_low)], axis=1)

    router_rows = jnp.transpose(w_router, (2, 0, 1)).reshape(OWN_TOKENS, 256)

    first_expert = 4 * c + 2 * r
    expert_range = jnp.arange(32, dtype=jnp.int32)[None, :]
    routers = None
    records = []
    normed = normed_first
    scale_one = None
    for layer in range(layers):
        partial, saved = attention_forward(normed, heads[layer], out_rows[layer], cosine, sine)
        middle = hidden + reduce_tokens(partial)
        scale_two, rows = norm_forward(middle, gains[2 * layer + 1])
        if layer == 0:
            normed_two, extra = gather_tokens(rows, router_rows)
            table = extra.reshape(2, 8, OWN_TOKENS, 256).reshape(2, 32, 2, HALF)
            table = jnp.where(lower, table, table[::-1])
            routers = [
                jnp.concatenate([table[0, :, i], table[1, :, i]], axis=1) for i in range(layers)
            ]
        else:
            normed_two = gather_tokens(rows)
        all_gates = gates_of(normed_two, routers[layer], expert_ids[layer])
        gates = [
            jnp.sum(jnp.where(expert_range == first_expert + e, all_gates, 0.0), 1, keepdims=True)
            for e in range(2)
        ]
        partial, pre = experts_forward(normed_two, gates, *ups[layer], *downs[layer])
        mixed = reduce_tokens(partial)
        result = middle + mixed
        records.append(
            dict(
                hidden=hidden,
                scale_one=scale_one,
                normed_one=normed,
                saved=saved,
                middle=middle,
                scale_two=scale_two,
                normed_two=normed_two,
                gates=gates,
                pre=pre,
                mixed=mixed,
            )
        )
        hidden = result
        if layer + 1 < layers:
            scale_one, rows = norm_forward(result, gains[2 * layer + 2])
            normed = gather_tokens(rows)

    def mean_columns(grad_rows, mixed_rows):
        high, low = split_two(jnp.sum(grad_rows * mixed_rows, axis=1, keepdims=True))
        return jnp.concatenate([high, low, jnp.zeros((OWN_TOKENS, 126), BF16)], axis=1)

    def mean_of(extra):
        flat = extra.reshape(TOKENS, 128).astype(F32)
        return flat[:, :1] + flat[:, 1:2]

    def spread_halves(rows, extra=None):
        low_half, high_half = rows[:, :HALF].astype(BF16), rows[:, HALF:].astype(BF16)
        if extra is not None:
            low_half = jnp.concatenate([low_half, extra], axis=1)
            high_half = jnp.concatenate([high_half, extra], axis=1)
        width = low_half.shape[1]
        send = jnp.concatenate(
            [
                jnp.broadcast_to(low_half[None], (8, OWN_TOKENS, width)),
                jnp.broadcast_to(high_half[None], (8, OWN_TOKENS, width)),
            ]
        )
        got = lax.all_to_all(send, GROUP, 0, 0, tiled=True)
        return got.reshape(TOKENS, width)

    got = spread_halves(hidden, mean_columns(grad_tokens, records[-1]["mixed"]))
    block_out = got[:, :HALF].astype(F32)
    mean = mean_of(got[:, HALF:])

    packs, smalls = [None] * layers, [None] * layers
    gain_sums = [None] * 4
    for layer in reversed(range(layers)):
        rec = records[layer]
        grad_normed, grad_logits, pack = experts_back(
            rec["normed_two"], rec["gates"], rec["pre"], *ups[layer], *downs[layer], upstream, mean
        )
        packs[layer] = lax.psum_scatter(pack, "dp", scatter_dimension=0, tiled=True)
        dense = jnp.zeros((TOKENS, 32), F32)
        for e in range(2):
            dense = jnp.where(expert_range == first_expert + e, grad_logits[e].astype(F32), dense)
        grad_normed = grad_normed + mm(dense.astype(BF16), routers[layer])
        local_ids = 4 * c + jnp.arange(4, dtype=jnp.int32)[None, :]
        local = jnp.zeros((TOKENS, 4), F32)
        for e in range(2):
            local = jnp.where(local_ids == first_expert + e, grad_logits[e].astype(F32), local)
        grad_router = mm_tn(rec["normed_two"], local.astype(BF16))
        total = reduce_tokens(grad_normed.astype(BF16))
        gain_two = gains[2 * layer + 1]
        grad_middle = grad_tokens + norm_back(rec["middle"], rec["scale_two"], gain_two, total)
        gain_part = jnp.sum(total * rec["middle"] * rec["scale_two"], axis=0)
        grad_low, extra = gather_tokens(grad_middle.astype(BF16), pack_vector(gain_part))
        gain_sums[2 * layer + 1] = unpack_vector(jnp.sum(extra.astype(F32), axis=0))
        grad_normed, grad_heads, grad_out = attention_back(
            rec["saved"], rec["normed_one"], grad_low, heads[layer], out_rows[layer], cosine, sine
        )
        gain_one = gains[2 * layer]
        gain_part = jnp.sum(grad_heads * heads[layer].astype(F32), axis=1)
        gain_part = own_first(gain_part) / gain_one
        total, extra = reduce_tokens(grad_normed, pack_vector(gain_part))
        gain_sums[2 * layer] = unpack_vector(extra)
        scale_one = rec["scale_one"]
        if layer == 0:
            scale_one = lax.rsqrt(
                jnp.mean(rec["hidden"] * rec["hidden"], axis=1, keepdims=True) + NORM_EPS
            )
        grad_tokens = grad_middle + norm_back(rec["hidden"], scale_one, gain_one, total)
        if layer > 0:
            upstream, extra = gather_tokens(
                grad_tokens.astype(BF16), mean_columns(grad_tokens, records[layer - 1]["mixed"])
            )
            mean = mean_of(extra)
        zero = jnp.zeros((MODEL_WIDTH, HEAD_SIZE), F32)
        q_grad = grad_heads[:, :HEAD_SIZE]
        q_wide = jnp.where(
            lower,
            jnp.concatenate([q_grad, zero], axis=1),
            jnp.concatenate([zero, q_grad], axis=1),
        )
        head_part = jnp.concatenate([q_wide, grad_heads[:, HEAD_SIZE:]], axis=1)
        head_part = head_part.reshape(2, N_DP, 64, 256)
        gain_cols = jnp.zeros((MODEL_WIDTH, 4), F32)
        if layer == 0:
            gain_cols = jnp.stack([0.5 * own_first(g) for g in gain_sums], axis=1)
        tail_part = jnp.concatenate(
            [grad_router, gain_cols, jnp.zeros((MODEL_WIDTH, 120), F32)], axis=1
        ).reshape(2, N_DP, 64, 128)
        zero = jnp.zeros_like(grad_out)
        out_part = jnp.where(
            lower,
            jnp.concatenate([grad_out, zero], axis=0),
            jnp.concatenate([zero, grad_out], axis=0),
        )
        out_part = out_part.reshape(N_DP, 16, 2, 4, 128).transpose(2, 0, 3, 1, 4)
        out_part = out_part.reshape(2, N_DP, 64, 128)
        part = jnp.concatenate([head_part, out_part, tail_part], axis=3).astype(BF16)
        smalls[layer] = part.transpose(1, 0, 2, 3)

    got = spread_halves(grad_tokens)
    grad_hidden = got.astype(F32)

    grads = []
    for layer in range(layers):
        if layer == 0:
            got = lax.all_to_all(
                smalls[layer].reshape(N_DP, 128, 512), "dp", 0, 0, tiled=True
            ).astype(F32)
            mine_small = jnp.sum(got, axis=0)
        else:
            mine_small = lax.psum_scatter(
                smalls[layer].reshape(N_DP, 128, 512), "dp", scatter_dimension=0, tiled=True
            ).astype(F32)[0]
        big = packs[layer][0]
        sent = jnp.concatenate([mine_small[64:].astype(BF16)], axis=0)
        total = mine_small[:64] + row_swap(sent).astype(F32)
        grad_qkv = total[:, :256]
        grad_out = total[:, 256:384].reshape(4, 16, 128).transpose(1, 0, 2).reshape(16, HALF)
        grad_router = total[:, 384:388]
        gain_grad = total[:, 388:392]
        up_pieces = big[:256].reshape(2, 2, 64, MODEL_WIDTH)
        down_pieces = big[256:].reshape(2, 64, MODEL_WIDTH)
        up_other = row_swap(up_pieces[:, 1])
        down_other = row_swap(down_pieces[:, :, HALF:])
        up_mine, down_mine = up_pieces[:, 0], down_pieces[:, :, :HALF]
        grad_up = jnp.where(
            lower,
            jnp.concatenate([up_mine, up_other]),
            jnp.concatenate([up_other, up_mine]),
        ).astype(F32)
        grad_down = jnp.where(
            lower,
            jnp.concatenate([down_mine, down_other]),
            jnp.concatenate([down_other, down_mine]),
        ).astype(F32)
        grads.append((gain_grad, grad_qkv, grad_out, grad_router, grad_up, grad_down))
    gain_out = grads[0][0].T.reshape(2, 2, 64)
    return (block_out, grad_hidden, gain_out) + tuple(
        jnp.stack([grads[layer][i] for layer in range(layers)]) for i in range(1, 6)
    )


def solution(mesh):
    placed = (
        P("dp", "row"),
        P("dp", "row"),
        P(None, None, "row"),
        P(None, "row", "col"),
        P(None, "col", "row"),
        P(None, "row", "col"),
        P(None, "col", "row", None),
        P(None, "col", None, "row"),
        P(None, "dp", None),
    )
    return jax.shard_map(
        body,
        mesh=mesh,
        in_specs=placed,
        out_specs=(
            P("dp", "row"),
            P("dp", "row"),
            P(None, None, ("row", "dp")),
            P(None, ("row", "dp"), "col"),
            P(None, ("col", "dp"), "row"),
            P(None, ("row", "dp"), "col"),
            P(None, "col", ("row", "dp"), None),
            P(None, "col", "dp", "row"),
        ),
        check_vma=False,
    )
```

```python
import jax
import jax.numpy as jnp
from jax import lax
from jax.experimental import pallas as pl
from jax.experimental.pallas import tpu as pltpu
from jax.sharding import PartitionSpec as P

MODEL_WIDTH = 1024
HALF = 512
HEAD_SIZE = 64
FF = 512
TOKENS = 256
PEERS = 16
OWN_TOKENS = 16
N_DP = 8
NORM_EPS = 1e-06
ROPE_BASE = 10000.0
GROUP = ("row", "col")
F32 = jnp.float32
BF16 = jnp.bfloat16


def dot(a, b, dims):
    return lax.dot_general(a, b, (dims, ((), ())), preferred_element_type=F32)


def mm(a, b):
    return dot(a, b, ((1,), (0,)))


def mm_nt(a, b):
    return dot(a, b, ((1,), (1,)))


def mm_tn(a, b):
    return dot(a, b, ((0,), (0,)))


def row_swap(value):
    return lax.ppermute(value, "row", [(0, 1), (1, 0)])


def swap_halves(value):
    return jnp.concatenate([value[..., HALF:MODEL_WIDTH], value[..., :HALF]], axis=-1)


def split_two(value):
    high = lax.reduce_precision(value, 8, 7)
    return (high.astype(BF16), (value - high).astype(BF16))


def rope_tables():
    half_width = HEAD_SIZE // 2
    frequency = ROPE_BASE ** (-2.0 * jnp.arange(half_width, dtype=F32) / HEAD_SIZE)
    angles = jnp.arange(TOKENS, dtype=F32)[:, None] * frequency[None, :]
    return (jnp.tile(jnp.cos(angles), (1, 4)), jnp.tile(jnp.sin(angles), (1, 4)))


def halves_swapped(pair, sign):
    lane = lax.broadcasted_iota(jnp.int32, pair.shape, 1) % HEAD_SIZE
    half = HEAD_SIZE // 2
    up = pltpu.roll(pair, 128 - half, 1)
    down = pltpu.roll(pair, half, 1)
    return jnp.where(lane < half, -sign * up, sign * down)


def causal():
    return lax.broadcasted_iota(jnp.int32, (TOKENS, TOKENS), 0) >= lax.broadcasted_iota(
        jnp.int32, (TOKENS, TOKENS), 1
    )


def whole(shape):
    zeros = (0,) * len(shape)
    return pl.BlockSpec(shape, lambda *_: zeros)


def at_layer(shape, layer):
    zeros = (0,) * (len(shape))
    return pl.BlockSpec((None,) + shape, lambda *_: (layer,) + zeros)


def shaped(shape, dtype):
    return jax.ShapeDtypeStruct(shape, dtype)


def cost(flops, size):
    return pl.CostEstimate(flops=flops, bytes_accessed=size, transcendentals=0)


def tokens_of(ref):
    return ref[:, :, :MODEL_WIDTH].reshape(TOKENS, MODEL_WIDTH)


def attend_kernel(x_ref, heads_ref, out_ref, cos_ref, sin_ref, part_ref, qkv_ref, att_ref, lse_ref):
    qkv = mm(tokens_of(x_ref), heads_ref[...])
    pair = qkv[:, :128]
    pair = (pair * cos_ref[...] + halves_swapped(pair, 1.0) * sin_ref[...]).astype(BF16)
    value = qkv[:, 128:].astype(BF16)
    scores = mm_nt(pair[:, :HEAD_SIZE], pair[:, HEAD_SIZE:]) * (1.0 / HEAD_SIZE)
    allowed = causal()
    total = jnp.log(jnp.sum(jnp.where(allowed, jnp.exp(scores), 0.0), axis=1, keepdims=True))
    probs = jnp.where(allowed, jnp.exp(scores - total), 0.0).astype(BF16)
    attended = mm(probs, value).astype(BF16)
    part = mm(attended, out_ref[...]).astype(BF16)
    part_ref[...] = part.reshape(PEERS, OWN_TOKENS, MODEL_WIDTH)
    qkv_ref[:, :128] = pair
    qkv_ref[:, 128:] = value
    att_ref[...] = attended
    lse_ref[...] = total


def attend(got, heads, out_rows, cosine, sine, layer):
    return pl.pallas_call(
        attend_kernel,
        name="attend",
        grid=(1,),
        in_specs=[
            whole(got.shape),
            at_layer(heads.shape[1:], layer),
            at_layer(out_rows.shape[1:], layer),
            whole(cosine.shape),
            whole(sine.shape),
        ],
        out_specs=[
            whole((PEERS, OWN_TOKENS, MODEL_WIDTH)),
            whole((TOKENS, 192)),
            whole((TOKENS, HEAD_SIZE)),
            whole((TOKENS, 1)),
        ],
        out_shape=[
            shaped((PEERS, OWN_TOKENS, MODEL_WIDTH), BF16),
            shaped((TOKENS, 192), BF16),
            shaped((TOKENS, HEAD_SIZE), BF16),
            shaped((TOKENS, 1), F32),
        ],
        cost_estimate=cost(200_000_000, 2_000_000),
    )(got, heads, out_rows, cosine, sine)


def attend_back_kernel(
    row_ref, low_ref, x_ref, heads_ref, out_ref, cos_ref, sin_ref, qkv_ref, att_ref, lse_ref,
    router_ref, gain_ref, send_ref, small_ref, sum_ref, pair_ref, cols_ref,
):
    lower = row_ref[0] == 0
    low = tokens_of(low_ref)
    sum_ref[...] = jnp.sum(low_ref[:, :, MODEL_WIDTH:].astype(F32), axis=0)
    query, key = qkv_ref[:, :HEAD_SIZE], qkv_ref[:, HEAD_SIZE:128]
    value = qkv_ref[:, 128:]
    attended = att_ref[...]
    grad_attended = mm_nt(low, out_ref[...]).astype(BF16)
    grad_out = mm_tn(attended, low)
    scores = mm_nt(query, key) * (1.0 / HEAD_SIZE)
    probs = jnp.where(causal(), jnp.exp(scores - lse_ref[...]), 0.0)
    grad_value = mm_tn(probs.astype(BF16), grad_attended)
    grad_probs = mm_nt(grad_attended, value)
    delta = jnp.sum(grad_attended.astype(F32) * attended.astype(F32), axis=1, keepdims=True)
    grad_scores = (probs * (grad_probs - delta) * (1.0 / HEAD_SIZE)).astype(BF16)
    pair_ref[:, :HEAD_SIZE] = mm(grad_scores, key)
    pair_ref[:, HEAD_SIZE:] = mm_tn(grad_scores, query)
    pair = pair_ref[...]
    pair = pair * cos_ref[...] + halves_swapped(pair * sin_ref[...], -1.0)
    cols_ref[:, :128] = pair.astype(BF16)
    cols_ref[:, 128:] = grad_value.astype(BF16)
    columns = cols_ref[...]
    part = mm_nt(columns, heads_ref[...]).astype(BF16)
    send_ref[:, :, :MODEL_WIDTH] = part.reshape(PEERS, OWN_TOKENS, MODEL_WIDTH)
    grad_heads = mm_tn(tokens_of(x_ref), columns)
    product = grad_heads * heads_ref[...].astype(F32)
    gain = lax.dot_general(
        jnp.ones((8, 192), F32),
        product,
        (((1,), (1,)), ((), ())),
        preferred_element_type=F32,
        precision=lax.Precision.HIGHEST,
    )[:1]
    gain = jnp.where(lower, gain, swap_halves(gain)) / gain_ref[...]
    high = gain.astype(BF16)
    rest = (gain - high.astype(F32)).astype(BF16)
    for j in range(8):
        lanes = slice(128 * j, 128 * j + 128)
        wide = slice(MODEL_WIDTH, MODEL_WIDTH + 128)
        send_ref[:, j : j + 1, wide] = jnp.broadcast_to(high[:, lanes][None], (PEERS, 1, 128))
        send_ref[:, 8 + j : 9 + j, wide] = jnp.broadcast_to(rest[:, lanes][None], (PEERS, 1, 128))
    query_part = grad_heads[:, :HEAD_SIZE].astype(BF16)
    rest_part = grad_heads[:, HEAD_SIZE:].astype(BF16)
    blank = jnp.zeros_like(query_part)
    slot_a = jnp.where(lower, query_part, blank)
    slot_b = jnp.where(lower, blank, query_part)
    router = router_ref[...].astype(BF16)
    grad_out = grad_out.astype(BF16)
    for k in range(N_DP):
        mine = (k // 4 == 0) == lower
        small_ref[k, 128:, :] = jnp.zeros((16, 512), BF16)
        for half in range(2):
            rows = slice(half * HALF + 64 * k, half * HALF + 64 * k + 64)
            to = slice(64 * half, 64 * half + 64)
            small_ref[k, to, :64] = slot_a[rows]
            small_ref[k, to, 64:128] = slot_b[rows]
            small_ref[k, to, 128:256] = rest_part[rows]
            small_ref[k, to, 384:] = jnp.zeros((64, 128), BF16)
            small_ref[k, to, 384:416] = router[rows]
            for j in range(4):
                piece = grad_out[16 * (k % 4) : 16 * (k % 4) + 16]
                piece = piece[:, half * HALF + 128 * j : half * HALF + 128 * j + 128]
                small_ref[k, 64 * half + 16 * j : 64 * half + 16 * j + 16, 256:384] = jnp.where(
                    mine, piece, jnp.zeros_like(piece)
                )


def attend_back(row, low, got, heads, out_rows, cosine, sine, saved, router_grad, gain, layer):
    qkv, attended, total = saved
    send = (PEERS, OWN_TOKENS, MODEL_WIDTH + 128)
    return pl.pallas_call(
        attend_back_kernel,
        name="attend_back",
        grid_spec=pltpu.PrefetchScalarGridSpec(
            num_scalar_prefetch=1,
            grid=(1,),
            in_specs=[
                whole(low.shape),
                whole(got.shape),
                at_layer(heads.shape[1:], layer),
                at_layer(out_rows.shape[1:], layer),
                whole(cosine.shape),
                whole(sine.shape),
                whole(qkv.shape),
                whole(attended.shape),
                whole(total.shape),
                whole(router_grad.shape),
                whole((1, MODEL_WIDTH)),
            ],
            out_specs=[whole(send), whole((N_DP, 144, 512)), whole((OWN_TOKENS, 128))],
            scratch_shapes=[pltpu.VMEM((TOKENS, 128), F32), pltpu.VMEM((TOKENS, 192), BF16)],
        ),
        out_shape=[
            shaped(send, BF16),
            shaped((N_DP, 144, 512), BF16),
            shaped((OWN_TOKENS, 128), F32),
        ],
        cost_estimate=cost(500_000_000, 4_000_000),
    )(row, low, got, heads, out_rows, cosine, sine, qkv, attended, total, router_grad, gain)


def gate_column(gates, first, step):
    experts = lax.broadcasted_iota(jnp.int32, gates.shape, 1)
    return jnp.sum(jnp.where(experts == first + step, gates, 0.0), axis=1, keepdims=True)


def experts_kernel(
    info_ref, x_ref, router_ref, ids_ref, up_ref, down_ref, other_ref,
    part_ref, pre_ref, gates_ref, sum_ref,
):
    step = pl.program_id(0)
    x = tokens_of(x_ref)

    @pl.when(step == 0)
    def _():
        logits = mm_nt(x, router_ref[...])
        experts = lax.broadcasted_iota(jnp.int32, logits.shape, 1)
        ids = ids_ref[...]
        chosen = ids[:, 0:1] == experts
        for j in range(1, 8):
            chosen = chosen | (ids[:, j : j + 1] == experts)
        exponent = jnp.where(chosen, jnp.exp(logits), 0.0)
        gates_ref[...] = exponent / jnp.sum(exponent, axis=1, keepdims=True)

    pre = mm(x[:, :HALF], up_ref[...]) + mm(x[:, HALF:], other_ref[:, : 2 * FF])
    pre_ref[...] = pre
    gate_part = pre[:, :FF]
    act = (gate_part / (1.0 + jnp.exp(-gate_part)) * pre[:, FF:]).astype(BF16)
    gate = gate_column(gates_ref[...], info_ref[1], step)
    left = gate * mm(act, down_ref[...])
    right = gate * mm(act, other_ref[:, 2 * FF :])

    @pl.when(step == 0)
    def _():
        sum_ref[:, :HALF] = left
        sum_ref[:, HALF:] = right

    @pl.when(step == 1)
    def _():
        shape = (PEERS, OWN_TOKENS, HALF)
        part_ref[:, :, :HALF] = (sum_ref[:, :HALF] + left).astype(BF16).reshape(shape)
        part_ref[:, :, HALF:] = (sum_ref[:, HALF:] + right).astype(BF16).reshape(shape)


def weight_specs(layer):
    return [
        pl.BlockSpec((None, None, HALF, 2 * FF), lambda e, info: (layer, 2 * info[0] + e, 0, 0)),
        pl.BlockSpec((None, None, FF, HALF), lambda e, info: (layer, 2 * info[0] + e, 0, 0)),
        pl.BlockSpec((HALF, 3 * HALF), lambda e, info: (e, 0)),
    ]


def experts(info, got, router, ids, w_up, w_down, other, layer):
    send = (PEERS, OWN_TOKENS, MODEL_WIDTH)
    return pl.pallas_call(
        experts_kernel,
        name="experts",
        grid_spec=pltpu.PrefetchScalarGridSpec(
            num_scalar_prefetch=1,
            grid=(2,),
            in_specs=[whole(got.shape), whole(router.shape), at_layer((TOKENS, 8), layer)]
            + weight_specs(layer),
            out_specs=[
                whole(send),
                pl.BlockSpec((None, TOKENS, 2 * FF), lambda e, info: (e, 0, 0)),
                whole((TOKENS, 32)),
            ],
            scratch_shapes=[pltpu.VMEM((TOKENS, MODEL_WIDTH), F32)],
        ),
        out_shape=[
            shaped(send, BF16),
            shaped((2, TOKENS, 2 * FF), F32),
            shaped((TOKENS, 32), F32),
        ],
        cost_estimate=cost(1_600_000_000, 9_000_000),
    )(info, got, router, ids, w_up, w_down, other)


def experts_back_kernel(
    info_ref, g_ref, mean_ref, gates_ref, pre_ref, router_ref, up_ref, down_ref, other_ref,
    part_ref, grad_pre_ref, act_ref, grad_y_ref, logit_ref, sum_ref,
):
    step = pl.program_id(0)
    upstream = g_ref[...]
    mean_cols = mean_ref[...].astype(F32)
    mean = mean_cols[:, :1] + mean_cols[:, 1:2]
    gates = gates_ref[...]
    gate = gate_column(gates, info_ref[1], step)
    gate_part, up_part = pre_ref[:, :FF], pre_ref[:, FF:]
    sig = 1.0 / (1.0 + jnp.exp(-gate_part))
    act = (gate_part * sig * up_part).astype(BF16)
    act_ref[...] = act
    raw = mm_nt(upstream[:, :HALF], down_ref[...])
    raw = raw + mm_nt(upstream[:, HALF:], other_ref[:, 2 * FF :])
    grad_gate = jnp.sum(act.astype(F32) * raw, axis=1, keepdims=True)
    back = gate * raw
    left = (back * up_part * sig * (1.0 + gate_part * (1.0 - sig))).astype(BF16)
    right = (back * gate_part * sig).astype(BF16)
    grad_pre_ref[:, :FF] = left
    grad_pre_ref[:, FF:] = right
    grad_pre = grad_pre_ref[...]
    grad_y_ref[...] = (gate * upstream.astype(F32)).astype(BF16)
    column = (gate * (grad_gate - mean)).astype(BF16).astype(F32)
    experts_at = lax.broadcasted_iota(jnp.int32, gates.shape, 1) == info_ref[1] + step
    low = mm_nt(grad_pre, up_ref[...])
    high = mm_nt(grad_pre, other_ref[:, : 2 * FF])

    @pl.when(step == 0)
    def _():
        logit_ref[...] = jnp.where(experts_at, column, 0.0)
        sum_ref[:, :HALF] = low
        sum_ref[:, HALF:] = high

    @pl.when(step == 1)
    def _():
        logits = jnp.where(experts_at, column, logit_ref[...])
        logit_ref[...] = logits
        routed = mm(logits.astype(BF16), router_ref[...])
        shape = (PEERS, OWN_TOKENS, HALF)
        low_sum = sum_ref[:, :HALF] + low + routed[:, :HALF]
        high_sum = sum_ref[:, HALF:] + high + routed[:, HALF:]
        part_ref[:, :, :HALF] = low_sum.astype(BF16).reshape(shape)
        part_ref[:, :, HALF:] = high_sum.astype(BF16).reshape(shape)


def experts_back(info, upstream, mean, gates, pre, router, w_up, w_down, other, layer):
    send = (PEERS, OWN_TOKENS, MODEL_WIDTH)

    def per_expert(width):
        return pl.BlockSpec((None, TOKENS, width), lambda e, info: (e, 0, 0))

    return pl.pallas_call(
        experts_back_kernel,
        name="experts_back",
        grid_spec=pltpu.PrefetchScalarGridSpec(
            num_scalar_prefetch=1,
            grid=(2,),
            in_specs=[
                whole(upstream.shape),
                whole(mean.shape),
                whole(gates.shape),
                per_expert(2 * FF),
                whole(router.shape),
            ]
            + weight_specs(layer),
            out_specs=[
                whole(send),
                per_expert(2 * FF),
                per_expert(FF),
                per_expert(MODEL_WIDTH),
                whole((TOKENS, 32)),
            ],
            scratch_shapes=[pltpu.VMEM((TOKENS, MODEL_WIDTH), F32)],
        ),
        out_shape=[
            shaped(send, BF16),
            shaped((2, TOKENS, 2 * FF), BF16),
            shaped((2, TOKENS, FF), BF16),
            shaped((2, TOKENS, MODEL_WIDTH), BF16),
            shaped((TOKENS, 32), F32),
        ],
        cost_estimate=cost(1_700_000_000, 11_000_000),
    )(info, upstream, mean, gates, pre, router, w_up, w_down, other)


def experts_grads_kernel(x_ref, grad_pre_ref, act_ref, grad_y_ref, logit_ref, pack_ref, router_ref):
    x = tokens_of(x_ref)
    up = mm_tn(x, grad_pre_ref[...]).astype(BF16)
    down = mm_tn(act_ref[...], grad_y_ref[...]).astype(BF16)
    for k in range(N_DP):
        pack_ref[k, :64] = up[64 * k : 64 * k + 64]
        pack_ref[k, 64:128] = up[HALF + 64 * k : HALF + 64 * k + 64]
        pack_ref[k, 128:] = down[64 * k : 64 * k + 64]

    @pl.when(pl.program_id(0) == 0)
    def _():
        router_ref[...] = mm_tn(x, logit_ref[...].astype(BF16))


def experts_grads(got, grad_pre, act, grad_y, logits):
    def per_expert(width):
        return pl.BlockSpec((None, TOKENS, width), lambda e: (e, 0, 0))

    return pl.pallas_call(
        experts_grads_kernel,
        name="experts_grads",
        grid=(2,),
        in_specs=[
            whole(got.shape),
            per_expert(2 * FF),
            per_expert(FF),
            per_expert(MODEL_WIDTH),
            whole(logits.shape),
        ],
        out_specs=[
            pl.BlockSpec((N_DP, 192, MODEL_WIDTH), lambda e: (0, e, 0)),
            whole((MODEL_WIDTH, 32)),
        ],
        out_shape=[shaped((N_DP, 384, MODEL_WIDTH), BF16), shaped((MODEL_WIDTH, 32), F32)],
        cost_estimate=cost(1_600_000_000, 9_000_000),
    )(got, grad_pre, act, grad_y, logits)


def summed(got_ref):
    first = got_ref[0, :, :MODEL_WIDTH].astype(F32)
    second = got_ref[8, :, :MODEL_WIDTH].astype(F32)
    for j in range(1, 8):
        first = first + got_ref[j, :, :MODEL_WIDTH].astype(F32)
        second = second + got_ref[8 + j, :, :MODEL_WIDTH].astype(F32)
    return first + swap_halves(second)


def put_rows(send_ref, rows):
    rows = rows.astype(BF16)
    swapped = swap_halves(rows)
    for j in range(8):
        send_ref[j, :, :MODEL_WIDTH] = rows
        send_ref[8 + j, :, :MODEL_WIDTH] = swapped


def put_halves(send_ref, rows):
    rows = rows.astype(BF16)
    for j in range(8):
        send_ref[j, :, :HALF] = rows[:, :HALF]
        send_ref[8 + j, :, :HALF] = rows[:, HALF:]


def put_extra(send_ref, extra, start):
    for j in range(PEERS):
        send_ref[j, :, start:] = extra


def pair_columns(column):
    high = column.astype(BF16).astype(F32)
    lane = lax.broadcasted_iota(jnp.int32, (OWN_TOKENS, 128), 1)
    wide = jnp.where(lane == 0, high, jnp.where(lane == 1, column - high, 0.0))
    return wide.astype(BF16)


def scale_of(hidden):
    return lax.rsqrt(jnp.mean(hidden * hidden, axis=1, keepdims=True) + NORM_EPS)


def add_norm_kernel(got_ref, base_ref, gain_ref, *rest):
    *extra, total_ref, sum_ref, send_ref = rest
    part = summed(got_ref)
    total = base_ref[...] + part
    total_ref[...] = total
    sum_ref[...] = part
    put_rows(send_ref, total * scale_of(total) * gain_ref[...])
    if extra:
        put_extra(send_ref, extra[0][...], MODEL_WIDTH)


def add_norm(got, base, gain, extra=None):
    width = MODEL_WIDTH + (0 if extra is None else extra.shape[1])
    rows = shaped((OWN_TOKENS, MODEL_WIDTH), F32)
    return pl.pallas_call(
        add_norm_kernel,
        name="add_norm",
        out_shape=[rows, rows, shaped((PEERS, OWN_TOKENS, width), BF16)],
        cost_estimate=cost(1_000_000, 1_000_000),
    )(got, base, gain, *([] if extra is None else [extra]))


def add_last_kernel(got_ref, base_ref, grad_ref, sum_ref, send_ref):
    part = summed(got_ref)
    sum_ref[...] = part
    put_halves(send_ref, base_ref[...] + part)
    mean = jnp.sum(grad_ref[...] * part, axis=1, keepdims=True)
    put_extra(send_ref, pair_columns(mean), HALF)


def add_last(got, base, grad):
    return pl.pallas_call(
        add_last_kernel,
        name="add_last",
        out_shape=[
            shaped((OWN_TOKENS, MODEL_WIDTH), F32),
            shaped((PEERS, OWN_TOKENS, HALF + 128), BF16),
        ],
        cost_estimate=cost(1_000_000, 1_000_000),
    )(got, base, grad)


def back_through_norm(hidden, gain, grad_normed):
    scaling = scale_of(hidden)
    weighted = grad_normed * gain
    inner = jnp.sum(weighted * hidden, axis=1, keepdims=True)
    return scaling * weighted - hidden * (scaling**3 * inner * (1.0 / MODEL_WIDTH))


def middle_back_kernel(got_ref, hidden_ref, gain_ref, grad_ref, out_ref, send_ref):
    grad_normed = summed(got_ref)
    hidden = hidden_ref[...]
    grad = grad_ref[...] + back_through_norm(hidden, gain_ref[...], grad_normed)
    out_ref[...] = grad
    put_rows(send_ref, grad)
    gain = jnp.sum(grad_normed * hidden * scale_of(hidden), axis=0, keepdims=True)
    high = gain.astype(BF16)
    rest = (gain - high.astype(F32)).astype(BF16)
    wide = slice(MODEL_WIDTH, MODEL_WIDTH + 128)
    for j in range(8):
        lanes = slice(128 * j, 128 * j + 128)
        send_ref[:, j : j + 1, wide] = jnp.broadcast_to(high[:, lanes][None], (PEERS, 1, 128))
        send_ref[:, 8 + j : 9 + j, wide] = jnp.broadcast_to(rest[:, lanes][None], (PEERS, 1, 128))


def middle_back(got, hidden, gain, grad):
    return pl.pallas_call(
        middle_back_kernel,
        name="middle_back",
        out_shape=[
            shaped((OWN_TOKENS, MODEL_WIDTH), F32),
            shaped((PEERS, OWN_TOKENS, MODEL_WIDTH + 128), BF16),
        ],
        cost_estimate=cost(1_000_000, 1_000_000),
    )(got, hidden, gain, grad)


def first_back_kernel(got_ref, hidden_ref, gain_ref, grad_ref, *rest):
    *mixed, out_ref, sum_ref, send_ref = rest
    hidden = hidden_ref[...]
    grad = grad_ref[...] + back_through_norm(hidden, gain_ref[...], summed(got_ref))
    out_ref[...] = grad
    sum_ref[...] = jnp.sum(got_ref[:, :, MODEL_WIDTH:].astype(F32), axis=0)
    if mixed:
        put_rows(send_ref, grad)
        mean = jnp.sum(grad * mixed[0][...], axis=1, keepdims=True)
        put_extra(send_ref, pair_columns(mean), MODEL_WIDTH)
    else:
        put_halves(send_ref, grad)


def first_back(got, hidden, gain, grad, mixed=None):
    width = HALF if mixed is None else MODEL_WIDTH + 128
    return pl.pallas_call(
        first_back_kernel,
        name="first_back",
        out_shape=[
            shaped((OWN_TOKENS, MODEL_WIDTH), F32),
            shaped((OWN_TOKENS, 128), F32),
            shaped((PEERS, OWN_TOKENS, width), BF16),
        ],
        cost_estimate=cost(1_000_000, 1_000_000),
    )(got, hidden, gain, grad, *([] if mixed is None else [mixed]))


def exchange(blocks):
    return lax.all_to_all(blocks, GROUP, 0, 0, tiled=True)


def body(
    hidden_in,
    cotangent,
    norm_gains,
    query_key_value_weight,
    w_out,
    w_router,
    w_gate_up,
    w_down,
    expert_ids,
):
    r = lax.axis_index("row")
    c = lax.axis_index("col")
    lower = r == 0
    layers = 2

    def natural(own, other):
        return jnp.where(
            lower,
            jnp.concatenate([own, other], axis=-1),
            jnp.concatenate([other, own], axis=-1),
        )

    cosine, sine = rope_tables()

    gain_first = norm_gains[0, 0]
    square = jnp.sum(hidden_in * hidden_in, axis=1, keepdims=True)
    high, low = split_two(square)
    sent = jnp.concatenate(
        [
            (hidden_in * gain_first).astype(BF16),
            high,
            low,
            jnp.zeros((TOKENS, 126), BF16),
        ],
        axis=1,
    )
    got = row_swap(sent)
    square = square + got[:, HALF : HALF + 1].astype(F32) + got[:, HALF + 1 : HALF + 2].astype(F32)
    scale_all = lax.rsqrt(square / MODEL_WIDTH + NORM_EPS)
    normed_first = jnp.concatenate(
        [hidden_in * scale_all * gain_first, got[:, :HALF].astype(F32) * scale_all], axis=1
    ).astype(BF16)

    q_low = query_key_value_weight[:, :, :HEAD_SIZE]
    q_high = query_key_value_weight[:, :, HEAD_SIZE : 2 * HEAD_SIZE]
    kv = query_key_value_weight[:, :, 2 * HEAD_SIZE :]
    heads_own = jnp.concatenate([jnp.where(lower, q_low, q_high), kv], axis=2)
    heads_sent = jnp.concatenate([jnp.where(lower, q_high, q_low), kv], axis=2)
    heads = jnp.concatenate([heads_own, row_swap(heads_sent)], axis=1)
    out_low, out_high = w_out[:, :HEAD_SIZE], w_out[:, HEAD_SIZE:]
    out_rows = jnp.concatenate(
        [jnp.where(lower, out_low, out_high), row_swap(jnp.where(lower, out_high, out_low))], axis=2
    )

    mine = (r * 8 + c) * OWN_TOKENS
    theirs = ((1 - r) * 8 + c) * OWN_TOKENS
    gains_flat = norm_gains.reshape(4, HALF)
    small = jnp.concatenate(
        [
            lax.dynamic_slice(hidden_in, (theirs, 0), (OWN_TOKENS, HALF)),
            lax.dynamic_slice(cotangent, (theirs, 0), (OWN_TOKENS, HALF)),
            gains_flat,
            jnp.zeros((4, HALF), F32),
        ]
    )
    small = row_swap(small)
    hidden = natural(
        lax.dynamic_slice(hidden_in, (mine, 0), (OWN_TOKENS, HALF)), small[:OWN_TOKENS]
    )
    grad_tokens = natural(
        lax.dynamic_slice(cotangent, (mine, 0), (OWN_TOKENS, HALF)),
        small[OWN_TOKENS : 2 * OWN_TOKENS],
    )
    gains = natural(gains_flat, small[2 * OWN_TOKENS : 2 * OWN_TOKENS + 4])

    k = lax.axis_index("dp")
    others = []
    for layer in range(layers):
        up_sent = lax.dynamic_slice(w_gate_up, (layer, 2 - 2 * r + k // 4, 128 * (k % 4), 0), (1, 1, 128, 2 * FF))
        down_sent = lax.dynamic_slice(w_down, (layer, 2 - 2 * r + k // 4, 128 * (k % 4), 0), (1, 1, 128, HALF))
        piece = row_swap(jnp.concatenate([up_sent[0, 0], down_sent[0, 0]], axis=1))
        others.append(lax.all_gather(piece, "dp", axis=0, tiled=True))
    cot_low = cotangent.astype(BF16)
    upstream = jnp.concatenate([cot_low, row_swap(cot_low)], axis=1)

    router_rows = jnp.transpose(w_router, (0, 2, 1)).reshape(OWN_TOKENS, 256)

    row = jnp.reshape(r, (1,))
    info = jnp.stack([r, 4 * c + 2 * r])
    gain_rows = [gains[i : i + 1] for i in range(4)]
    routers = None
    records = []
    rows_in = normed_first.reshape(PEERS, OWN_TOKENS, MODEL_WIDTH)
    for layer in range(layers):
        partial, *saved = attend(rows_in, heads, out_rows, cosine, sine, layer)
        got = exchange(partial)
        if layer == 0:
            middle, _, send = add_norm(got, hidden, gain_rows[1], router_rows)
            got = exchange(send)
            table = got[:, :, MODEL_WIDTH:].reshape(2, 8, 2, 4, HALF)
            table = jnp.where(lower, table, table[::-1])
            table = jnp.transpose(table, (2, 1, 3, 0, 4)).reshape(2, 32, MODEL_WIDTH)
            routers = [table[0], table[1]]
        else:
            middle, _, send = add_norm(got, hidden, gain_rows[2 * layer + 1])
            got = exchange(send)
        normed_two = got
        partial, pre, gates = experts(
            info, normed_two, routers[layer], expert_ids, w_gate_up, w_down, others[layer], layer
        )
        got = exchange(partial)
        rec = dict(hidden=hidden, normed_one=rows_in, saved=saved, middle=middle)
        rec.update(normed_two=normed_two, gates=gates, pre=pre)
        if layer + 1 < layers:
            hidden, mixed, send = add_norm(got, middle, gain_rows[2 * layer + 2])
            rows_in = exchange(send)
        else:
            mixed, send = add_last(got, middle, grad_tokens)
            got = exchange(send).reshape(TOKENS, HALF + 128)
            block_out = got[:, :HALF].astype(F32)
            mean = got[:, HALF:]
        rec.update(mixed=mixed)
        records.append(rec)

    packs, smalls = [None] * layers, [None] * layers
    gain_sums = [None] * 4
    for layer in reversed(range(layers)):
        rec = records[layer]
        partial, grad_pre, act, grad_y, grad_logits = experts_back(
            info, upstream, mean, rec["gates"], rec["pre"], routers[layer],
            w_gate_up, w_down, others[layer], layer,
        )
        got = exchange(partial)
        pack, router_grad = experts_grads(rec["normed_two"], grad_pre, act, grad_y, grad_logits)
        packs[layer] = lax.psum_scatter(pack, "dp", scatter_dimension=0, tiled=True)
        grad_middle, send = middle_back(got, rec["middle"], gain_rows[2 * layer + 1], grad_tokens)
        low = exchange(send)
        send, smalls[layer], gain_sums[2 * layer + 1] = attend_back(
            row, low, rec["normed_one"], heads, out_rows, cosine, sine, rec["saved"],
            router_grad, gain_rows[2 * layer], layer,
        )
        got = exchange(send)
        if layer > 0:
            grad_tokens, gain_sums[2 * layer], send = first_back(
                got, rec["hidden"], gain_rows[2 * layer], grad_middle, records[layer - 1]["mixed"]
            )
            got = exchange(send)
            upstream = got[:, :, :MODEL_WIDTH].reshape(TOKENS, MODEL_WIDTH)
            mean = got[:, :, MODEL_WIDTH:].reshape(TOKENS, 128)
        else:
            _, gain_sums[0], send = first_back(got, rec["hidden"], gain_rows[0], grad_middle)
            grad_hidden = exchange(send).reshape(TOKENS, HALF).astype(F32)

    gain_flat = jnp.concatenate([g[:8] + g[8:] for g in gain_sums], axis=1)
    high, low = split_two(gain_flat)
    gain_block = jnp.broadcast_to(jnp.concatenate([high, low])[None], (N_DP, 16, 512))
    smalls[0] = lax.dynamic_update_slice(smalls[0], gain_block, (0, 128, 0))

    grads = []
    for layer in range(layers):
        if layer == 0:
            got = lax.all_to_all(smalls[layer], "dp", 0, 0, tiled=True).astype(F32)
            mine_small = jnp.sum(got, axis=0)
            flat = (mine_small[128:136] + mine_small[136:]).reshape(8, 4, 128)
            flat = lax.dynamic_index_in_dim(flat, 4 * r + k // 2, 0, keepdims=False)
            flat = flat.reshape(4, 2, 64)
            gain_out = lax.dynamic_index_in_dim(flat, k % 2, 1, keepdims=False).reshape(2, 2, 64)
        else:
            mine_small = lax.psum_scatter(smalls[layer], "dp", scatter_dimension=0, tiled=True)
            mine_small = mine_small[0].astype(F32)
        big = packs[layer][0]
        total = mine_small[:64] + row_swap(mine_small[64:128].astype(BF16)).astype(F32)
        grad_qkv = total[:, :256]
        grad_out = total[:, 256:384].reshape(4, 16, 128).transpose(1, 0, 2).reshape(16, HALF)
        grad_router = lax.dynamic_slice(total, (0, 384 + 4 * c), (64, 4))
        big = big.reshape(2, 192, MODEL_WIDTH)
        up_pieces = big[:, :128].reshape(2, 2, 64, MODEL_WIDTH)
        down_pieces = big[:, 128:]
        up_other = row_swap(up_pieces[:, 1])
        down_other = row_swap(down_pieces[:, :, HALF:])
        up_mine, down_mine = up_pieces[:, 0], down_pieces[:, :, :HALF]
        grad_up = jnp.where(
            lower,
            jnp.concatenate([up_mine, up_other]),
            jnp.concatenate([up_other, up_mine]),
        ).astype(F32)
        grad_down = jnp.where(
            lower,
            jnp.concatenate([down_mine, down_other]),
            jnp.concatenate([down_other, down_mine]),
        ).astype(F32)
        grads.append((grad_qkv, grad_out, grad_router, grad_up, grad_down))
    return (block_out, grad_hidden, gain_out) + tuple(
        jnp.stack([grads[layer][i] for layer in range(layers)]) for i in range(5)
    )


def solution(mesh):
    placed = (
        P("dp", "row"),
        P("dp", "row"),
        P(None, None, "row"),
        P(None, "row", "col"),
        P(None, "col", "row"),
        P(None, "row", "col"),
        P(None, "col", "row", None),
        P(None, "col", None, "row"),
        P(None, "dp", None),
    )
    return jax.shard_map(
        body,
        mesh=mesh,
        in_specs=placed,
        out_specs=(
            P("dp", "row"),
            P("dp", "row"),
            P(None, None, ("row", "dp")),
            P(None, ("row", "dp"), "col"),
            P(None, ("col", "dp"), "row"),
            P(None, ("row", "dp"), "col"),
            P(None, "col", ("row", "dp"), None),
            P(None, "col", "dp", "row"),
        ),
        check_vma=False,
    )
```

```python
import jax
import jax.numpy as jnp
from jax import lax
from jax.experimental import pallas as pl
from jax.experimental.pallas import tpu as pltpu
from jax.sharding import PartitionSpec as P

MODEL_WIDTH = 1024
HALF = 512
HEAD_SIZE = 64
FF = 512
TOKENS = 256
PEERS = 16
OWN_TOKENS = 16
N_DP = 8
NORM_EPS = 1e-06
ROPE_BASE = 10000.0
GROUP = ("row", "col")
F32 = jnp.float32
BF16 = jnp.bfloat16


def dot(a, b, dims):
    return lax.dot_general(a, b, (dims, ((), ())), preferred_element_type=F32)


def mm(a, b):
    return dot(a, b, ((1,), (0,)))


def mm_nt(a, b):
    return dot(a, b, ((1,), (1,)))


def mm_tn(a, b):
    return dot(a, b, ((0,), (0,)))


def row_swap(value):
    return lax.ppermute(value, "row", [(0, 1), (1, 0)])


def swap_halves(value):
    return jnp.concatenate([value[..., HALF:MODEL_WIDTH], value[..., :HALF]], axis=-1)


def split_two(value):
    high = lax.reduce_precision(value, 8, 7)
    return (high.astype(BF16), (value - high).astype(BF16))


def rope_tables():
    half_width = HEAD_SIZE // 2
    frequency = ROPE_BASE ** (-2.0 * jnp.arange(half_width, dtype=F32) / HEAD_SIZE)
    angles = jnp.arange(TOKENS, dtype=F32)[:, None] * frequency[None, :]
    return (jnp.tile(jnp.cos(angles), (1, 4)), jnp.tile(jnp.sin(angles), (1, 4)))


def halves_swapped(pair, sign):
    lane = lax.broadcasted_iota(jnp.int32, pair.shape, 1) % HEAD_SIZE
    half = HEAD_SIZE // 2
    up = pltpu.roll(pair, 128 - half, 1)
    down = pltpu.roll(pair, half, 1)
    return jnp.where(lane < half, -sign * up, sign * down)


def causal():
    return lax.broadcasted_iota(jnp.int32, (TOKENS, TOKENS), 0) >= lax.broadcasted_iota(
        jnp.int32, (TOKENS, TOKENS), 1
    )


def whole(shape):
    zeros = (0,) * len(shape)
    return pl.BlockSpec(shape, lambda *_: zeros)


def at_layer(shape, layer):
    zeros = (0,) * (len(shape))
    return pl.BlockSpec((None,) + shape, lambda *_: (layer,) + zeros)


def shaped(shape, dtype):
    return jax.ShapeDtypeStruct(shape, dtype)


def cost(flops, size):
    return pl.CostEstimate(flops=flops, bytes_accessed=size, transcendentals=0)


def tokens_of(ref):
    return ref[:, :, :MODEL_WIDTH].reshape(TOKENS, MODEL_WIDTH)


def attend_kernel(x_ref, heads_ref, out_ref, cos_ref, sin_ref, part_ref, qkv_ref, att_ref, lse_ref):
    qkv = mm(tokens_of(x_ref), heads_ref[...])
    pair = qkv[:, :128]
    pair = (pair * cos_ref[...] + halves_swapped(pair, 1.0) * sin_ref[...]).astype(BF16)
    value = qkv[:, 128:].astype(BF16)
    scores = mm_nt(pair[:, :HEAD_SIZE], pair[:, HEAD_SIZE:]) * (1.0 / HEAD_SIZE)
    allowed = causal()
    total = jnp.log(jnp.sum(jnp.where(allowed, jnp.exp(scores), 0.0), axis=1, keepdims=True))
    probs = jnp.where(allowed, jnp.exp(scores - total), 0.0).astype(BF16)
    attended = mm(probs, value).astype(BF16)
    part = mm(attended, out_ref[...]).astype(BF16)
    part_ref[...] = part.reshape(PEERS, OWN_TOKENS, MODEL_WIDTH)
    qkv_ref[:, :128] = pair
    qkv_ref[:, 128:] = value
    att_ref[...] = attended
    lse_ref[...] = total


def attend(got, heads, out_rows, cosine, sine):
    return pl.pallas_call(
        attend_kernel,
        name="attend",
        grid=(1,),
        in_specs=[
            whole(got.shape),
            whole(heads.shape),
            whole(out_rows.shape),
            whole(cosine.shape),
            whole(sine.shape),
        ],
        out_specs=[
            whole((PEERS, OWN_TOKENS, MODEL_WIDTH)),
            whole((TOKENS, 192)),
            whole((TOKENS, HEAD_SIZE)),
            whole((TOKENS, 1)),
        ],
        out_shape=[
            shaped((PEERS, OWN_TOKENS, MODEL_WIDTH), BF16),
            shaped((TOKENS, 192), BF16),
            shaped((TOKENS, HEAD_SIZE), BF16),
            shaped((TOKENS, 1), F32),
        ],
        cost_estimate=cost(200_000_000, 2_000_000),
    )(got, heads, out_rows, cosine, sine)


def attend_back_kernel(
    row_ref, low_ref, x_ref, heads_ref, out_ref, cos_ref, sin_ref, qkv_ref, att_ref, lse_ref,
    router_ref, gain_ref, send_ref, small_ref, sum_ref, pair_ref, cols_ref,
):
    lower = row_ref[0] == 0
    low = tokens_of(low_ref)
    sum_ref[...] = jnp.sum(low_ref[:, :, MODEL_WIDTH:].astype(F32), axis=0)
    query, key = qkv_ref[:, :HEAD_SIZE], qkv_ref[:, HEAD_SIZE:128]
    value = qkv_ref[:, 128:]
    attended = att_ref[...]
    grad_attended = mm_nt(low, out_ref[...]).astype(BF16)
    grad_out = mm_tn(attended, low)
    scores = mm_nt(query, key) * (1.0 / HEAD_SIZE)
    probs = jnp.where(causal(), jnp.exp(scores - lse_ref[...]), 0.0)
    grad_value = mm_tn(probs.astype(BF16), grad_attended)
    grad_probs = mm_nt(grad_attended, value)
    delta = jnp.sum(grad_attended.astype(F32) * attended.astype(F32), axis=1, keepdims=True)
    grad_scores = (probs * (grad_probs - delta) * (1.0 / HEAD_SIZE)).astype(BF16)
    pair_ref[:, :HEAD_SIZE] = mm(grad_scores, key)
    pair_ref[:, HEAD_SIZE:] = mm_tn(grad_scores, query)
    pair = pair_ref[...]
    pair = pair * cos_ref[...] + halves_swapped(pair * sin_ref[...], -1.0)
    cols_ref[:, :128] = pair.astype(BF16)
    cols_ref[:, 128:] = grad_value.astype(BF16)
    columns = cols_ref[...]
    part = mm_nt(columns, heads_ref[...]).astype(BF16)
    send_ref[:, :, :MODEL_WIDTH] = part.reshape(PEERS, OWN_TOKENS, MODEL_WIDTH)
    grad_heads = mm_tn(tokens_of(x_ref), columns)
    product = grad_heads * heads_ref[...].astype(F32)
    gain = lax.dot_general(
        jnp.ones((8, 192), F32),
        product,
        (((1,), (1,)), ((), ())),
        preferred_element_type=F32,
        precision=lax.Precision.HIGHEST,
    )[:1]
    gain = jnp.where(lower, gain, swap_halves(gain)) / gain_ref[...]
    high = gain.astype(BF16)
    rest = (gain - high.astype(F32)).astype(BF16)
    for j in range(8):
        lanes = slice(128 * j, 128 * j + 128)
        wide = slice(MODEL_WIDTH, MODEL_WIDTH + 128)
        send_ref[:, j : j + 1, wide] = jnp.broadcast_to(high[:, lanes][None], (PEERS, 1, 128))
        send_ref[:, 8 + j : 9 + j, wide] = jnp.broadcast_to(rest[:, lanes][None], (PEERS, 1, 128))
    query_part = grad_heads[:, :HEAD_SIZE].astype(BF16)
    rest_part = grad_heads[:, HEAD_SIZE:].astype(BF16)
    blank = jnp.zeros_like(query_part)
    slot_a = jnp.where(lower, query_part, blank)
    slot_b = jnp.where(lower, blank, query_part)
    router = router_ref[...].astype(BF16)
    grad_out = grad_out.astype(BF16)
    for k in range(N_DP):
        mine = (k // 4 == 0) == lower
        small_ref[k, 128:, :] = jnp.zeros((16, 512), BF16)
        for half in range(2):
            rows = slice(half * HALF + 64 * k, half * HALF + 64 * k + 64)
            to = slice(64 * half, 64 * half + 64)
            small_ref[k, to, :64] = slot_a[rows]
            small_ref[k, to, 64:128] = slot_b[rows]
            small_ref[k, to, 128:256] = rest_part[rows]
            small_ref[k, to, 384:] = jnp.zeros((64, 128), BF16)
            small_ref[k, to, 384:416] = router[rows]
            for j in range(4):
                piece = grad_out[16 * (k % 4) : 16 * (k % 4) + 16]
                piece = piece[:, half * HALF + 128 * j : half * HALF + 128 * j + 128]
                small_ref[k, 64 * half + 16 * j : 64 * half + 16 * j + 16, 256:384] = jnp.where(
                    mine, piece, jnp.zeros_like(piece)
                )


def attend_back(row, low, got, heads, out_rows, cosine, sine, saved, router_grad, gain):
    qkv, attended, total = saved
    send = (PEERS, OWN_TOKENS, MODEL_WIDTH + 128)
    return pl.pallas_call(
        attend_back_kernel,
        name="attend_back",
        grid_spec=pltpu.PrefetchScalarGridSpec(
            num_scalar_prefetch=1,
            grid=(1,),
            in_specs=[
                whole(low.shape),
                whole(got.shape),
                whole(heads.shape),
                whole(out_rows.shape),
                whole(cosine.shape),
                whole(sine.shape),
                whole(qkv.shape),
                whole(attended.shape),
                whole(total.shape),
                whole(router_grad.shape),
                whole((1, MODEL_WIDTH)),
            ],
            out_specs=[whole(send), whole((N_DP, 144, 512)), whole((OWN_TOKENS, 128))],
            scratch_shapes=[pltpu.VMEM((TOKENS, 128), F32), pltpu.VMEM((TOKENS, 192), BF16)],
        ),
        out_shape=[
            shaped(send, BF16),
            shaped((N_DP, 144, 512), BF16),
            shaped((OWN_TOKENS, 128), F32),
        ],
        cost_estimate=cost(500_000_000, 4_000_000),
    )(row, low, got, heads, out_rows, cosine, sine, qkv, attended, total, router_grad, gain)


def gate_column(gates, first, step):
    experts = lax.broadcasted_iota(jnp.int32, gates.shape, 1)
    return jnp.sum(jnp.where(experts == first + step, gates, 0.0), axis=1, keepdims=True)


def experts_kernel(
    info_ref, x_ref, router_ref, ids_ref, up_ref, down_ref, other_ref,
    part_ref, pre_ref, gates_ref, sum_ref,
):
    step = pl.program_id(0)
    x = tokens_of(x_ref)

    @pl.when(step == 0)
    def _():
        logits = mm_nt(x, router_ref[...])
        experts = lax.broadcasted_iota(jnp.int32, logits.shape, 1)
        ids = ids_ref[...]
        chosen = ids[:, 0:1] == experts
        for j in range(1, 8):
            chosen = chosen | (ids[:, j : j + 1] == experts)
        exponent = jnp.where(chosen, jnp.exp(logits), 0.0)
        gates_ref[...] = exponent / jnp.sum(exponent, axis=1, keepdims=True)

    pre = mm(x[:, :HALF], up_ref[...]) + mm(x[:, HALF:], other_ref[:, : 2 * FF])
    pre_ref[...] = pre
    gate_part = pre[:, :FF]
    act = (gate_part / (1.0 + jnp.exp(-gate_part)) * pre[:, FF:]).astype(BF16)
    gate = gate_column(gates_ref[...], info_ref[1], step)
    left = gate * mm(act, down_ref[...])
    right = gate * mm(act, other_ref[:, 2 * FF :])

    @pl.when(step == 0)
    def _():
        sum_ref[:, :HALF] = left
        sum_ref[:, HALF:] = right

    @pl.when(step == 1)
    def _():
        shape = (PEERS, OWN_TOKENS, HALF)
        part_ref[:, :, :HALF] = (sum_ref[:, :HALF] + left).astype(BF16).reshape(shape)
        part_ref[:, :, HALF:] = (sum_ref[:, HALF:] + right).astype(BF16).reshape(shape)


def weight_specs(layer):
    return [
        pl.BlockSpec((None, None, HALF, 2 * FF), lambda e, info: (layer, 2 * info[0] + e, 0, 0)),
        pl.BlockSpec((None, None, FF, HALF), lambda e, info: (layer, 2 * info[0] + e, 0, 0)),
        pl.BlockSpec((HALF, 3 * HALF), lambda e, info: (e, 0)),
    ]


def experts(info, got, router, ids, w_up, w_down, other, layer):
    send = (PEERS, OWN_TOKENS, MODEL_WIDTH)
    return pl.pallas_call(
        experts_kernel,
        name="experts",
        grid_spec=pltpu.PrefetchScalarGridSpec(
            num_scalar_prefetch=1,
            grid=(2,),
            in_specs=[whole(got.shape), whole(router.shape), at_layer((TOKENS, 8), layer)]
            + weight_specs(layer),
            out_specs=[
                whole(send),
                pl.BlockSpec((None, TOKENS, 2 * FF), lambda e, info: (e, 0, 0)),
                whole((TOKENS, 32)),
            ],
            scratch_shapes=[pltpu.VMEM((TOKENS, MODEL_WIDTH), F32)],
        ),
        out_shape=[
            shaped(send, BF16),
            shaped((2, TOKENS, 2 * FF), F32),
            shaped((TOKENS, 32), F32),
        ],
        cost_estimate=cost(1_600_000_000, 9_000_000),
    )(info, got, router, ids, w_up, w_down, other)


def experts_back_kernel(
    info_ref, g_ref, mean_ref, gates_ref, pre_ref, router_ref, up_ref, down_ref, other_ref,
    part_ref, grad_pre_ref, act_ref, grad_y_ref, logit_ref, sum_ref,
):
    step = pl.program_id(0)
    upstream = g_ref[...]
    mean_cols = mean_ref[...].astype(F32)
    mean = mean_cols[:, :1] + mean_cols[:, 1:2]
    gates = gates_ref[...]
    gate = gate_column(gates, info_ref[1], step)
    gate_part, up_part = pre_ref[:, :FF], pre_ref[:, FF:]
    sig = 1.0 / (1.0 + jnp.exp(-gate_part))
    act = (gate_part * sig * up_part).astype(BF16)
    act_ref[...] = act
    raw = mm_nt(upstream[:, :HALF], down_ref[...])
    raw = raw + mm_nt(upstream[:, HALF:], other_ref[:, 2 * FF :])
    grad_gate = jnp.sum(act.astype(F32) * raw, axis=1, keepdims=True)
    back = gate * raw
    left = (back * up_part * sig * (1.0 + gate_part * (1.0 - sig))).astype(BF16)
    right = (back * gate_part * sig).astype(BF16)
    grad_pre_ref[:, :FF] = left
    grad_pre_ref[:, FF:] = right
    grad_pre = grad_pre_ref[...]
    grad_y_ref[...] = (gate * upstream.astype(F32)).astype(BF16)
    column = (gate * (grad_gate - mean)).astype(BF16).astype(F32)
    experts_at = lax.broadcasted_iota(jnp.int32, gates.shape, 1) == info_ref[1] + step
    low = mm_nt(grad_pre, up_ref[...])
    high = mm_nt(grad_pre, other_ref[:, : 2 * FF])

    @pl.when(step == 0)
    def _():
        logit_ref[...] = jnp.where(experts_at, column, 0.0)
        sum_ref[:, :HALF] = low
        sum_ref[:, HALF:] = high

    @pl.when(step == 1)
    def _():
        logits = jnp.where(experts_at, column, logit_ref[...])
        logit_ref[...] = logits
        routed = mm(logits.astype(BF16), router_ref[...])
        shape = (PEERS, OWN_TOKENS, HALF)
        low_sum = sum_ref[:, :HALF] + low + routed[:, :HALF]
        high_sum = sum_ref[:, HALF:] + high + routed[:, HALF:]
        part_ref[:, :, :HALF] = low_sum.astype(BF16).reshape(shape)
        part_ref[:, :, HALF:] = high_sum.astype(BF16).reshape(shape)


def experts_back(info, upstream, mean, gates, pre, router, w_up, w_down, other, layer):
    send = (PEERS, OWN_TOKENS, MODEL_WIDTH)

    def per_expert(width):
        return pl.BlockSpec((None, TOKENS, width), lambda e, info: (e, 0, 0))

    return pl.pallas_call(
        experts_back_kernel,
        name="experts_back",
        grid_spec=pltpu.PrefetchScalarGridSpec(
            num_scalar_prefetch=1,
            grid=(2,),
            in_specs=[
                whole(upstream.shape),
                whole(mean.shape),
                whole(gates.shape),
                per_expert(2 * FF),
                whole(router.shape),
            ]
            + weight_specs(layer),
            out_specs=[
                whole(send),
                per_expert(2 * FF),
                per_expert(FF),
                per_expert(MODEL_WIDTH),
                whole((TOKENS, 32)),
            ],
            scratch_shapes=[pltpu.VMEM((TOKENS, MODEL_WIDTH), F32)],
        ),
        out_shape=[
            shaped(send, BF16),
            shaped((2, TOKENS, 2 * FF), BF16),
            shaped((2, TOKENS, FF), BF16),
            shaped((2, TOKENS, MODEL_WIDTH), BF16),
            shaped((TOKENS, 32), F32),
        ],
        cost_estimate=cost(1_700_000_000, 11_000_000),
    )(info, upstream, mean, gates, pre, router, w_up, w_down, other)


def experts_grads_kernel(x_ref, grad_pre_ref, act_ref, grad_y_ref, logit_ref, pack_ref, router_ref):
    x = tokens_of(x_ref)
    up = mm_tn(x, grad_pre_ref[...]).astype(BF16)
    down = mm_tn(act_ref[...], grad_y_ref[...]).astype(BF16)
    for k in range(N_DP):
        pack_ref[k, :64] = up[64 * k : 64 * k + 64]
        pack_ref[k, 64:128] = up[HALF + 64 * k : HALF + 64 * k + 64]
        pack_ref[k, 128:] = down[64 * k : 64 * k + 64]

    @pl.when(pl.program_id(0) == 0)
    def _():
        router_ref[...] = mm_tn(x, logit_ref[...].astype(BF16))


def experts_grads(got, grad_pre, act, grad_y, logits):
    def per_expert(width):
        return pl.BlockSpec((None, TOKENS, width), lambda e: (e, 0, 0))

    return pl.pallas_call(
        experts_grads_kernel,
        name="experts_grads",
        grid=(2,),
        in_specs=[
            whole(got.shape),
            per_expert(2 * FF),
            per_expert(FF),
            per_expert(MODEL_WIDTH),
            whole(logits.shape),
        ],
        out_specs=[
            pl.BlockSpec((N_DP, 192, MODEL_WIDTH), lambda e: (0, e, 0)),
            whole((MODEL_WIDTH, 32)),
        ],
        out_shape=[shaped((N_DP, 384, MODEL_WIDTH), BF16), shaped((MODEL_WIDTH, 32), F32)],
        cost_estimate=cost(1_600_000_000, 9_000_000),
    )(got, grad_pre, act, grad_y, logits)


def summed(got_ref):
    first = got_ref[0, :, :MODEL_WIDTH].astype(F32)
    second = got_ref[8, :, :MODEL_WIDTH].astype(F32)
    for j in range(1, 8):
        first = first + got_ref[j, :, :MODEL_WIDTH].astype(F32)
        second = second + got_ref[8 + j, :, :MODEL_WIDTH].astype(F32)
    return first + swap_halves(second)


def put_rows(send_ref, rows):
    rows = rows.astype(BF16)
    swapped = swap_halves(rows)
    for j in range(8):
        send_ref[j, :, :MODEL_WIDTH] = rows
        send_ref[8 + j, :, :MODEL_WIDTH] = swapped


def put_halves(send_ref, rows):
    rows = rows.astype(BF16)
    for j in range(8):
        send_ref[j, :, :HALF] = rows[:, :HALF]
        send_ref[8 + j, :, :HALF] = rows[:, HALF:]


def put_extra(send_ref, extra, start):
    for j in range(PEERS):
        send_ref[j, :, start:] = extra


def pair_columns(column):
    high = column.astype(BF16).astype(F32)
    lane = lax.broadcasted_iota(jnp.int32, (OWN_TOKENS, 128), 1)
    wide = jnp.where(lane == 0, high, jnp.where(lane == 1, column - high, 0.0))
    return wide.astype(BF16)


def scale_of(hidden):
    return lax.rsqrt(jnp.mean(hidden * hidden, axis=1, keepdims=True) + NORM_EPS)


def add_norm_kernel(got_ref, base_ref, gain_ref, *rest):
    *extra, total_ref, sum_ref, send_ref = rest
    part = summed(got_ref)
    total = base_ref[...] + part
    total_ref[...] = total
    sum_ref[...] = part
    put_rows(send_ref, total * scale_of(total) * gain_ref[...])
    if extra:
        put_extra(send_ref, extra[0][...], MODEL_WIDTH)


def add_norm(got, base, gain, extra=None):
    width = MODEL_WIDTH + (0 if extra is None else extra.shape[1])
    rows = shaped((OWN_TOKENS, MODEL_WIDTH), F32)
    return pl.pallas_call(
        add_norm_kernel,
        name="add_norm",
        out_shape=[rows, rows, shaped((PEERS, OWN_TOKENS, width), BF16)],
        cost_estimate=cost(1_000_000, 1_000_000),
    )(got, base, gain, *([] if extra is None else [extra]))


def add_last_kernel(got_ref, base_ref, grad_ref, sum_ref, send_ref):
    part = summed(got_ref)
    sum_ref[...] = part
    put_halves(send_ref, base_ref[...] + part)
    mean = jnp.sum(grad_ref[...] * part, axis=1, keepdims=True)
    put_extra(send_ref, pair_columns(mean), HALF)


def add_last(got, base, grad):
    return pl.pallas_call(
        add_last_kernel,
        name="add_last",
        out_shape=[
            shaped((OWN_TOKENS, MODEL_WIDTH), F32),
            shaped((PEERS, OWN_TOKENS, HALF + 128), BF16),
        ],
        cost_estimate=cost(1_000_000, 1_000_000),
    )(got, base, grad)


def back_through_norm(hidden, gain, grad_normed):
    scaling = scale_of(hidden)
    weighted = grad_normed * gain
    inner = jnp.sum(weighted * hidden, axis=1, keepdims=True)
    return scaling * weighted - hidden * (scaling**3 * inner * (1.0 / MODEL_WIDTH))


def middle_back_kernel(got_ref, hidden_ref, gain_ref, grad_ref, out_ref, send_ref):
    grad_normed = summed(got_ref)
    hidden = hidden_ref[...]
    grad = grad_ref[...] + back_through_norm(hidden, gain_ref[...], grad_normed)
    out_ref[...] = grad
    put_rows(send_ref, grad)
    gain = jnp.sum(grad_normed * hidden * scale_of(hidden), axis=0, keepdims=True)
    high = gain.astype(BF16)
    rest = (gain - high.astype(F32)).astype(BF16)
    wide = slice(MODEL_WIDTH, MODEL_WIDTH + 128)
    for j in range(8):
        lanes = slice(128 * j, 128 * j + 128)
        send_ref[:, j : j + 1, wide] = jnp.broadcast_to(high[:, lanes][None], (PEERS, 1, 128))
        send_ref[:, 8 + j : 9 + j, wide] = jnp.broadcast_to(rest[:, lanes][None], (PEERS, 1, 128))


def middle_back(got, hidden, gain, grad):
    return pl.pallas_call(
        middle_back_kernel,
        name="middle_back",
        out_shape=[
            shaped((OWN_TOKENS, MODEL_WIDTH), F32),
            shaped((PEERS, OWN_TOKENS, MODEL_WIDTH + 128), BF16),
        ],
        cost_estimate=cost(1_000_000, 1_000_000),
    )(got, hidden, gain, grad)


def first_back_kernel(got_ref, hidden_ref, gain_ref, grad_ref, *rest):
    *mixed, out_ref, sum_ref, send_ref = rest
    hidden = hidden_ref[...]
    grad = grad_ref[...] + back_through_norm(hidden, gain_ref[...], summed(got_ref))
    out_ref[...] = grad
    sum_ref[...] = jnp.sum(got_ref[:, :, MODEL_WIDTH:].astype(F32), axis=0)
    if mixed:
        put_rows(send_ref, grad)
        mean = jnp.sum(grad * mixed[0][...], axis=1, keepdims=True)
        put_extra(send_ref, pair_columns(mean), MODEL_WIDTH)
    else:
        put_halves(send_ref, grad)


def first_back(got, hidden, gain, grad, mixed=None):
    width = HALF if mixed is None else MODEL_WIDTH + 128
    return pl.pallas_call(
        first_back_kernel,
        name="first_back",
        out_shape=[
            shaped((OWN_TOKENS, MODEL_WIDTH), F32),
            shaped((OWN_TOKENS, 128), F32),
            shaped((PEERS, OWN_TOKENS, width), BF16),
        ],
        cost_estimate=cost(1_000_000, 1_000_000),
    )(got, hidden, gain, grad, *([] if mixed is None else [mixed]))


def after(value):
    return (value.reshape(-1)[0].astype(F32) > 1e30).astype(jnp.int32)


def exchange(blocks):
    return lax.all_to_all(blocks, GROUP, 0, 0, tiled=True)


def body(
    hidden_in,
    cotangent,
    norm_gains,
    query_key_value_weight,
    w_out,
    w_router,
    w_gate_up,
    w_down,
    expert_ids,
):
    r = lax.axis_index("row")
    c = lax.axis_index("col")
    lower = r == 0
    layers = 2

    def natural(own, other):
        return jnp.where(
            lower,
            jnp.concatenate([own, other], axis=-1),
            jnp.concatenate([other, own], axis=-1),
        )

    cosine, sine = rope_tables()

    gain_first = norm_gains[0, 0]
    square = jnp.sum(hidden_in * hidden_in, axis=1, keepdims=True)
    high, low = split_two(square)
    sent = jnp.concatenate(
        [
            (hidden_in * gain_first).astype(BF16),
            high,
            low,
            jnp.zeros((TOKENS, 126), BF16),
        ],
        axis=1,
    )
    got = row_swap(sent)
    square = square + got[:, HALF : HALF + 1].astype(F32) + got[:, HALF + 1 : HALF + 2].astype(F32)
    scale_all = lax.rsqrt(square / MODEL_WIDTH + NORM_EPS)
    normed_first = jnp.concatenate(
        [hidden_in * scale_all * gain_first, got[:, :HALF].astype(F32) * scale_all], axis=1
    ).astype(BF16)

    def attention_weights(layer, index):
        first = index == 0
        columns = query_key_value_weight[layer]
        q_low, q_high = columns[:, :HEAD_SIZE], columns[:, HEAD_SIZE : 2 * HEAD_SIZE]
        kv = columns[:, 2 * HEAD_SIZE :]
        own = jnp.concatenate([jnp.where(first, q_low, q_high), kv], axis=1)
        sent = jnp.concatenate([jnp.where(first, q_high, q_low), kv], axis=1)
        low, high = w_out[layer, :HEAD_SIZE], w_out[layer, HEAD_SIZE:]
        out_other = row_swap(jnp.where(first, high, low))
        return (
            jnp.concatenate([own, row_swap(sent)], axis=0),
            jnp.concatenate([jnp.where(first, low, high), out_other], axis=1),
        )

    mine = (r * 8 + c) * OWN_TOKENS
    theirs = ((1 - r) * 8 + c) * OWN_TOKENS
    gains_flat = norm_gains.reshape(4, HALF)
    small = jnp.concatenate(
        [
            lax.dynamic_slice(hidden_in, (theirs, 0), (OWN_TOKENS, HALF)),
            lax.dynamic_slice(cotangent, (theirs, 0), (OWN_TOKENS, HALF)),
            gains_flat,
            jnp.zeros((4, HALF), F32),
        ]
    )
    small = row_swap(small)
    hidden = natural(
        lax.dynamic_slice(hidden_in, (mine, 0), (OWN_TOKENS, HALF)), small[:OWN_TOKENS]
    )
    grad_tokens = natural(
        lax.dynamic_slice(cotangent, (mine, 0), (OWN_TOKENS, HALF)),
        small[OWN_TOKENS : 2 * OWN_TOKENS],
    )
    gains = natural(gains_flat, small[2 * OWN_TOKENS : 2 * OWN_TOKENS + 4])

    k = lax.axis_index("dp")

    def other_weights(layer, index):
        start = (layer, 2 - 2 * index + k // 4, 128 * (k % 4), 0)
        up_sent = lax.dynamic_slice(w_gate_up, start, (1, 1, 128, 2 * FF))
        down_sent = lax.dynamic_slice(w_down, start, (1, 1, 128, HALF))
        piece = row_swap(jnp.concatenate([up_sent[0, 0], down_sent[0, 0]], axis=1))
        return lax.all_gather(piece, "dp", axis=0, tiled=True)

    weights = [attention_weights(0, r), None]
    others = [other_weights(0, r + after(square)), None]

    router_rows = jnp.transpose(w_router, (0, 2, 1)).reshape(OWN_TOKENS, 256)

    row = jnp.reshape(r, (1,))
    info = jnp.stack([r, 4 * c + 2 * r])
    gain_rows = [gains[i : i + 1] for i in range(4)]
    routers = None
    records = []
    rows_in = normed_first.reshape(PEERS, OWN_TOKENS, MODEL_WIDTH)
    for layer in range(layers):
        partial, *saved = attend(rows_in, *weights[layer], cosine, sine)
        got = exchange(partial)
        if layer == 0:
            middle, _, send = add_norm(got, hidden, gain_rows[1], router_rows)
            got = exchange(send)
            table = got[:, :, MODEL_WIDTH:].reshape(2, 8, 2, 4, HALF)
            table = jnp.where(lower, table, table[::-1])
            table = jnp.transpose(table, (2, 1, 3, 0, 4)).reshape(2, 32, MODEL_WIDTH)
            routers = [table[0], table[1]]
        else:
            middle, _, send = add_norm(got, hidden, gain_rows[2 * layer + 1])
            got = exchange(send)
        normed_two = got
        if layer == 0:
            index = r + after(got[0, :1, :1])
            weights[1] = attention_weights(1, index)
            others[1] = other_weights(1, index)
            cot_low = cotangent.astype(BF16)
            cot_low = lax.dynamic_slice(cot_low, (index - r, 0), (TOKENS, HALF))
            upstream = jnp.concatenate([cot_low, row_swap(cot_low)], axis=1)
        partial, pre, gates = experts(
            info, normed_two, routers[layer], expert_ids, w_gate_up, w_down, others[layer], layer
        )
        got = exchange(partial)
        rec = dict(hidden=hidden, normed_one=rows_in, saved=saved, middle=middle)
        rec.update(normed_two=normed_two, gates=gates, pre=pre)
        if layer + 1 < layers:
            hidden, mixed, send = add_norm(got, middle, gain_rows[2 * layer + 2])
            rows_in = exchange(send)
        else:
            mixed, send = add_last(got, middle, grad_tokens)
            got = exchange(send).reshape(TOKENS, HALF + 128)
            block_out = got[:, :HALF].astype(F32)
            mean = got[:, HALF:]
        rec.update(mixed=mixed)
        records.append(rec)

    def big_grads(pack):
        big = lax.psum_scatter(pack, "dp", scatter_dimension=0, tiled=True)[0]
        big = big.reshape(2, 192, MODEL_WIDTH)
        up_pieces = big[:, :128].reshape(2, 2, 64, MODEL_WIDTH)
        down_pieces = big[:, 128:]
        up_other = row_swap(up_pieces[:, 1])
        down_other = row_swap(down_pieces[:, :, HALF:])
        arrived = after(up_other[0, :1, :1]) + after(down_other[0, :1, :1])
        return up_pieces[:, 0], up_other, down_pieces[:, :, :HALF], down_other, arrived

    packs, smalls = [None] * layers, [None] * layers
    gain_sums = [None] * 4
    for layer in reversed(range(layers)):
        rec = records[layer]
        partial, grad_pre, act, grad_y, grad_logits = experts_back(
            info, upstream, mean, rec["gates"], rec["pre"], routers[layer],
            w_gate_up, w_down, others[layer], layer,
        )
        got = exchange(partial)
        pack, router_grad = experts_grads(rec["normed_two"], grad_pre, act, grad_y, grad_logits)
        packs[layer] = big_grads(pack)
        if layer == 0:
            row = row + packs[1][-1]
        grad_middle, send = middle_back(got, rec["middle"], gain_rows[2 * layer + 1], grad_tokens)
        low = exchange(send)
        send, smalls[layer], gain_sums[2 * layer + 1] = attend_back(
            row, low, rec["normed_one"], *weights[layer], cosine, sine, rec["saved"],
            router_grad, gain_rows[2 * layer],
        )
        got = exchange(send)
        if layer > 0:
            grad_tokens, gain_sums[2 * layer], send = first_back(
                got, rec["hidden"], gain_rows[2 * layer], grad_middle, records[layer - 1]["mixed"]
            )
            got = exchange(send)
            upstream = got[:, :, :MODEL_WIDTH].reshape(TOKENS, MODEL_WIDTH)
            mean = got[:, :, MODEL_WIDTH:].reshape(TOKENS, 128)
        else:
            _, gain_sums[0], send = first_back(got, rec["hidden"], gain_rows[0], grad_middle)
            grad_hidden = exchange(send).reshape(TOKENS, HALF).astype(F32)

    gain_flat = jnp.concatenate([g[:8] + g[8:] for g in gain_sums], axis=1)
    high, low = split_two(gain_flat)
    gain_block = jnp.broadcast_to(jnp.concatenate([high, low])[None], (N_DP, 16, 512))
    smalls[0] = lax.dynamic_update_slice(smalls[0], gain_block, (0, 128, 0))

    grads = []
    for layer in range(layers):
        if layer == 0:
            got = lax.all_to_all(smalls[layer], "dp", 0, 0, tiled=True).astype(F32)
            mine_small = jnp.sum(got, axis=0)
            flat = (mine_small[128:136] + mine_small[136:]).reshape(8, 4, 128)
            flat = lax.dynamic_index_in_dim(flat, 4 * r + k // 2, 0, keepdims=False)
            flat = flat.reshape(4, 2, 64)
            gain_out = lax.dynamic_index_in_dim(flat, k % 2, 1, keepdims=False).reshape(2, 2, 64)
        else:
            mine_small = lax.psum_scatter(smalls[layer], "dp", scatter_dimension=0, tiled=True)
            mine_small = mine_small[0].astype(F32)
        up_mine, up_other, down_mine, down_other, arrived = packs[layer]
        sent = lax.dynamic_slice(mine_small, (64 + arrived, 0), (64, 512)).astype(BF16)
        total = mine_small[:64] + row_swap(sent).astype(F32)
        grad_qkv = total[:, :256]
        grad_out = total[:, 256:384].reshape(4, 16, 128).transpose(1, 0, 2).reshape(16, HALF)
        grad_router = lax.dynamic_slice(total, (0, 384 + 4 * c), (64, 4))
        grad_up = jnp.where(
            lower,
            jnp.concatenate([up_mine, up_other]),
            jnp.concatenate([up_other, up_mine]),
        ).astype(F32)
        grad_down = jnp.where(
            lower,
            jnp.concatenate([down_mine, down_other]),
            jnp.concatenate([down_other, down_mine]),
        ).astype(F32)
        grads.append((grad_qkv, grad_out, grad_router, grad_up, grad_down))
    return (block_out, grad_hidden, gain_out) + tuple(
        jnp.stack([grads[layer][i] for layer in range(layers)]) for i in range(5)
    )


def solution(mesh):
    placed = (
        P("dp", "row"),
        P("dp", "row"),
        P(None, None, "row"),
        P(None, "row", "col"),
        P(None, "col", "row"),
        P(None, "row", "col"),
        P(None, "col", "row", None),
        P(None, "col", None, "row"),
        P(None, "dp", None),
    )
    return jax.shard_map(
        body,
        mesh=mesh,
        in_specs=placed,
        out_specs=(
            P("dp", "row"),
            P("dp", "row"),
            P(None, None, ("row", "dp")),
            P(None, ("row", "dp"), "col"),
            P(None, ("col", "dp"), "row"),
            P(None, ("row", "dp"), "col"),
            P(None, "col", ("row", "dp"), None),
            P(None, "col", "dp", "row"),
        ),
        check_vma=False,
    )
```
